32 devices in a mesh: rep: 4 (over y, core), fsdp: 8 (over z, x).
Axes of the slice: x: 2, y: 2, z: 4, core: 2. Of those that a mesh axis runs over, the one named last changes fastest.
Arguments:
- query_rows: bfloat16 [4, 3072, 2560], P('rep', 'fsdp'), may hold values from -5 to 5
- key_rows: bfloat16 [4, 3072, 2560], P('rep', 'fsdp'), may hold values from -5 to 5
- value_rows: bfloat16 [4, 3072, 2560], P('rep', 'fsdp'), may hold values from -5 to 5
- residual_in: bfloat16 [4, 3072, 2560], P('rep', 'fsdp'), may hold values from -6 to 6
- out_grad: bfloat16 [4, 3072, 2560], P('rep', 'fsdp'), may hold values from -6 to 6
- doc_ids: int32 [4, 3072], P('rep', 'fsdp'), may hold values from 0 to 47, never falling along the last dimension, each value on 1 to 256 neighbouring positions
- out_weight: bfloat16 [4, 2560, 2560], P('rep', 'fsdp'), may hold values from -0.125 to 0.125
- momentum: float32 [4, 2560, 2560], P('rep', 'fsdp'), may hold values from -192 to 192
- step_index: int32 [1], replicated, may hold values from 0 to 63
Outputs:
- block_out: bfloat16 [4, 3072, 2560], P('rep', 'fsdp')
- query_grad: bfloat16 [4, 3072, 2560], P('rep', 'fsdp')
- key_grad: bfloat16 [4, 3072, 2560], P('rep', 'fsdp')
- value_grad: bfloat16 [4, 3072, 2560], P('rep', 'fsdp')
- new_weight: bfloat16 [4, 2560, 2560], P('rep', 'fsdp')
- new_momentum: float32 [4, 2560, 2560], P('rep', 'fsdp')
The draws below stay inside these ranges and needn't reach their ends.
All inputs are finite; a program needn't handle non-finite values.
Results may differ from the reference program's by a relative error of at most 0.018.
Values may be sent and summed in bfloat16 or wider, within the bound.
A program may use at most 192 MiB of HBM per device.

```python
import math
import jax
import jax.numpy as jnp
import numpy as np
from jax import lax

D = 2560
HEADS = 20
HEAD_SIZE = 128
TOK_DEV = 384
HD = 2560
TOKENS = 3072
N_REP = 4


def query_key_pair(key):
    shape = (N_REP, TOKENS, HD)
    first = jax.random.fold_in(key, 11)
    second = jax.random.fold_in(key, 12)
    queries = jnp.clip(jax.random.normal(first, shape, jnp.float32), -5.0, 5.0)
    keyset = jnp.clip(jax.random.normal(second, shape, jnp.float32), -5.0, 5.0)
    return (queries, keyset)


def draw_query_rows(key, part):
    return query_key_pair(key)[0].astype(jnp.bfloat16)


def draw_key_rows(key, part):
    return query_key_pair(key)[1].astype(jnp.bfloat16)


def block_scale(own_key, extent, split, least, top_value):
    def one(position, blocks):
        heights = jax.random.uniform(jax.random.fold_in(jax.random.fold_in(own_key, 6), position), (blocks,), jnp.float32, least / len(split), top_value / len(split))
        return jnp.repeat(jnp.exp(heights), extent[position] // blocks).reshape((-1,) + (1,) * (len(extent) - position - 1))

    gain = one(*split[0])
    for cut in split[1:]:
        gain = gain * one(*cut)
    return gain


def length_profile(count, total, reach, lean):
    portions = [(1 << 20) // math.isqrt(rank ** lean) + 1 for rank in range(2, count + 1)]
    surplus, counts = total - reach - (count - 1), [1] * (count - 1)
    while surplus > 0:
        free = [i for i in range(count - 1) if counts[i] < reach]
        pool, left = sum([portions[i] for i in free]), surplus
        for i in free:
            addition = min(reach - counts[i], max(1, left * portions[i] // pool), surplus)
            counts[i] = counts[i] + addition
            surplus = surplus - addition
    return np.array([reach] + counts)


def uneven_parts(own_key, count, total, most, lean):
    if count == 2:
        one = jax.random.randint(own_key, (), max(1, total - most), min(most, total - 1) + 1)
        return jnp.stack([one, total - one])
    sizes = jnp.asarray(length_profile(count, total, most, lean), jnp.int32)
    couples = (count - 1) // 2
    source_of, taker = sizes[1:1 + 2 * couples:2], sizes[2:2 + 2 * couples:2]
    slack = jnp.minimum(source_of - 1, most - taker)
    moved = jax.random.randint(jax.random.fold_in(own_key, 1), (couples,), 0, 1 << 20) % (slack + 1)
    sizes = sizes.at[1:1 + 2 * couples:2].set(source_of - moved).at[2:2 + 2 * couples:2].set(taker + moved)
    return sizes[jax.random.permutation(jax.random.fold_in(own_key, 2), count)]


def bell_draw(own_key, dims, deviation, most, cuts=(), kind=jnp.bfloat16):
    values = deviation * jax.random.normal(own_key, dims, jnp.float32)
    if cuts:
        values = values * block_scale(own_key, dims, cuts, -0.22, 0.18)
    return jnp.clip(values, -most, most).astype(kind)


def setup_inputs(seed: int = 0) -> dict:
    streams_of = jax.random.split(jax.random.key(seed), 10)
    query_rows = draw_query_rows(jax.random.fold_in(streams_of[9], 71), 0)
    key_rows = draw_key_rows(jax.random.fold_in(streams_of[9], 71), 0)
    value_rows = bell_draw(streams_of[2], (N_REP, TOKENS, HD), 1.0, 5.0, ((0, 4), (1, 8)))
    residual_in = bell_draw(streams_of[3], (N_REP, TOKENS, D), 1.0, 6.0, ((0, 4), (1, 8)))
    out_grad = bell_draw(streams_of[4], (N_REP, TOKENS, D), 1.0, 6.0, ((0, 4), (1, 8)))
    doc_ids = jax.vmap(lambda own: jnp.searchsorted(jnp.cumsum(uneven_parts(own, max(4, TOKENS // 64), TOKENS, min(256, TOKENS // 2), 1)), jnp.arange(TOKENS), side="right"))(jax.random.split(streams_of[5], N_REP)).reshape((N_REP, TOKENS)).astype(jnp.int32)
    out_weight = bell_draw(streams_of[6], (N_REP, HD, D), HD ** -0.5, 0.125, ((0, 4), (1, 8)))
    momentum = bell_draw(streams_of[7], (N_REP, HD, D), 32.0, 192.0, ((0, 4), (1, 8)), jnp.float32)
    step_index = jax.random.randint(streams_of[8], (1,), 0, 64).astype(jnp.int32)
    return {"query_rows": query_rows, "key_rows": key_rows, "value_rows": value_rows, "residual_in": residual_in, "out_grad": out_grad, "doc_ids": doc_ids, "out_weight": out_weight, "momentum": momentum, "step_index": step_index}


momentum_decay = 0.9
learning_rate = 0.0003


def rounded(values):
    return lax.optimization_barrier(values.astype(jnp.bfloat16)).astype(jnp.float32)


def attend(query_block, key_block, value_block, doc_block):
    length = query_block.shape[0]
    score_scale = HEAD_SIZE ** -0.5
    query_heads = query_block.astype(jnp.float32).reshape(length, HEADS, HEAD_SIZE)
    key_heads = key_block.astype(jnp.float32).reshape(length, HEADS, HEAD_SIZE)
    value_heads = value_block.astype(jnp.float32).reshape(length, HEADS, HEAD_SIZE)
    scores = jnp.einsum("qhd,khd->hqk", query_heads, key_heads) * score_scale
    places = jnp.arange(length, dtype=jnp.int32)
    allowed = (places[None, :] <= places[:, None]) & (doc_block[:, None] == doc_block[None, :])
    scores = jnp.where(allowed[None], scores, -jnp.inf)
    row_peaks = jnp.max(scores, axis=-1, keepdims=True)
    exponents = jnp.exp(scores - row_peaks)
    attn_probs = exponents / jnp.sum(exponents, axis=-1, keepdims=True)
    probs_low = rounded(attn_probs)
    context = jnp.einsum("hqk,khd->qhd", probs_low, value_heads)
    context = context.reshape(length, HEADS * HEAD_SIZE).astype(jnp.bfloat16)
    return context, attn_probs, probs_low, query_heads, key_heads, value_heads


def attend_back(context_grad, attn_probs, probs_low, query_heads, key_heads, value_heads):
    length = query_heads.shape[0]
    score_scale = HEAD_SIZE ** -0.5
    grad_heads = context_grad.astype(jnp.float32).reshape(length, HEADS, HEAD_SIZE)
    value_grad = jnp.einsum("hqk,qhd->khd", probs_low, grad_heads)
    prob_grad = jnp.einsum("qhd,khd->hqk", grad_heads, value_heads)
    row_delta = jnp.sum(prob_grad * attn_probs, axis=-1, keepdims=True)
    score_grad = rounded(attn_probs * (prob_grad - row_delta) * score_scale)
    query_grad = jnp.einsum("hqk,khd->qhd", score_grad, key_heads)
    key_grad = jnp.einsum("hqk,qhd->khd", score_grad, query_heads)
    width = HEADS * HEAD_SIZE
    return (query_grad.reshape(length, width).astype(jnp.bfloat16),
            key_grad.reshape(length, width).astype(jnp.bfloat16),
            value_grad.reshape(length, width).astype(jnp.bfloat16))


def reference(query_rows, key_rows, value_rows, residual_in, out_grad, doc_ids, out_weight, momentum, step_index):
    hidden = HEADS * HEAD_SIZE
    blocks = TOKENS // TOK_DEV
    outputs_block, outputs_query, outputs_key, outputs_value = [], [], [], []
    moments, stepped_all = [], []
    for replica in range(N_REP):
        weight = out_weight[replica]

        def one_block(running, pieces):
            query_block, key_block, value_block, resid_block, grad_block, doc_block = pieces
            context, attn_probs, probs_low, query_heads, key_heads, value_heads = attend(query_block, key_block, value_block, doc_block)
            projected = jnp.dot(context, weight, preferred_element_type=jnp.float32)
            block_out = (resid_block.astype(jnp.float32) + projected).astype(jnp.bfloat16)
            context_grad = lax.dot_general(grad_block, weight, (((1,), (1,)), ((), ())), preferred_element_type=jnp.float32).astype(jnp.bfloat16)
            query_grad, key_grad, value_grad = attend_back(context_grad, attn_probs, probs_low, query_heads, key_heads, value_heads)
            weight_term = lax.dot_general(context, grad_block, (((0,), (0,)), ((), ())), preferred_element_type=jnp.float32)
            return running + rounded(weight_term), (block_out, query_grad, key_grad, value_grad)

        def per_block(array):
            return array[replica].reshape((blocks, TOK_DEV) + array.shape[2:])

        pieces = (per_block(query_rows), per_block(key_rows), per_block(value_rows),
                  per_block(residual_in), per_block(out_grad), per_block(doc_ids))
        weight_grad, results = lax.scan(one_block, jnp.zeros((hidden, D), jnp.float32), pieces)
        outputs_block.append(results[0].reshape(TOKENS, D))
        outputs_query.append(results[1].reshape(TOKENS, hidden))
        outputs_key.append(results[2].reshape(TOKENS, hidden))
        outputs_value.append(results[3].reshape(TOKENS, hidden))
        new_momentum = momentum_decay * momentum[replica] + weight_grad
        moments.append(new_momentum)
        stepped_all.append((weight.astype(jnp.float32) - learning_rate * new_momentum).astype(jnp.bfloat16))
    stepped = jnp.stack(stepped_all)
    levels = N_REP.bit_length() - 1
    chosen_level = (step_index[0] % levels).astype(jnp.int32)
    partner = jnp.bitwise_xor(jnp.arange(N_REP, dtype=jnp.int32), jnp.left_shift(jnp.ones((), jnp.int32), chosen_level))
    new_weight = ((stepped.astype(jnp.float32) + stepped[partner].astype(jnp.float32)) * 0.5).astype(jnp.bfloat16)
    return (jnp.stack(outputs_block), jnp.stack(outputs_query), jnp.stack(outputs_key),
            jnp.stack(outputs_value), new_weight, jnp.stack(moments))
```

```python
import functools

import jax
import jax.numpy as jnp
from jax import lax
from jax.experimental import pallas as pl
from jax.experimental.pallas import tpu as pltpu
from jax.sharding import PartitionSpec as P

HEAD_SIZE = 128

momentum_decay = 0.9
learning_rate = 0.0003


def swapped(block, axis, distance):
    count = lax.axis_size(axis)
    route = []
    for low in range(count):
        high = low | 1 << distance
        if high != low and high < count:
            route += [(low, high), (high, low)]
    return lax.ppermute(block, axis, route)


def probabilities(q, k, doc_column, doc_row):
    length = q.shape[0]
    scores = lax.dot_general(
        q, k, (((1,), (1,)), ((), ())), preferred_element_type=jnp.float32
    ) * (HEAD_SIZE ** (-0.5))
    rows = lax.broadcasted_iota(jnp.int32, (length, length), 0)
    columns = lax.broadcasted_iota(jnp.int32, (length, length), 1)
    allowed = (columns <= rows) & (doc_column == doc_row)
    scores = jnp.where(allowed, scores, -jnp.inf)
    exponents = jnp.exp(scores - jnp.max(scores, axis=-1, keepdims=True))
    return exponents / jnp.sum(exponents, axis=-1, keepdims=True)


def forward_kernel(q_ref, k_ref, v_ref, doc_column_ref, doc_row_ref, context_ref):
    for head in range(q_ref.shape[1] // HEAD_SIZE):
        cut = slice(head * HEAD_SIZE, (head + 1) * HEAD_SIZE)
        probs = probabilities(q_ref[:, cut], k_ref[:, cut], doc_column_ref[...], doc_row_ref[...])
        context_ref[:, cut] = jnp.dot(
            probs.astype(jnp.bfloat16), v_ref[:, cut], preferred_element_type=jnp.float32
        ).astype(jnp.bfloat16)


def backward_kernel(
    q_ref, k_ref, v_ref, grad_ref, doc_column_ref, doc_row_ref, dq_ref, dk_ref, dv_ref
):
    for head in range(q_ref.shape[1] // HEAD_SIZE):
        cut = slice(head * HEAD_SIZE, (head + 1) * HEAD_SIZE)
        q, k, v, grad = q_ref[:, cut], k_ref[:, cut], v_ref[:, cut], grad_ref[:, cut]
        probs = probabilities(q, k, doc_column_ref[...], doc_row_ref[...])
        dv_ref[:, cut] = lax.dot_general(
            probs.astype(jnp.bfloat16),
            grad,
            (((0,), (0,)), ((), ())),
            preferred_element_type=jnp.float32,
        ).astype(jnp.bfloat16)
        prob_grad = lax.dot_general(
            grad, v, (((1,), (1,)), ((), ())), preferred_element_type=jnp.float32
        )
        row_delta = jnp.sum(prob_grad * probs, axis=-1, keepdims=True)
        score_grad = (probs * (prob_grad - row_delta) * (HEAD_SIZE ** (-0.5))).astype(jnp.bfloat16)
        dq_ref[:, cut] = jnp.dot(score_grad, k, preferred_element_type=jnp.float32).astype(
            jnp.bfloat16
        )
        dk_ref[:, cut] = lax.dot_general(
            score_grad, q, (((0,), (0,)), ((), ())), preferred_element_type=jnp.float32
        ).astype(jnp.bfloat16)


def per_head(kernel, arrays, doc_block, outputs, matmuls):
    length, width = arrays[0].shape
    step = 2 * HEAD_SIZE if width % (2 * HEAD_SIZE) == 0 else HEAD_SIZE
    block = pl.BlockSpec((length, step), lambda h: (0, h))
    whole = lambda shape: pl.BlockSpec(shape, lambda h: (0, 0))
    result = jax.ShapeDtypeStruct((length, width), jnp.bfloat16)
    return pl.pallas_call(
        kernel,
        grid=(width // step,),
        in_specs=[block] * len(arrays) + [whole((length, 1)), whole((1, length))],
        out_specs=[block] * outputs,
        out_shape=[result] * outputs,
        cost_estimate=pl.CostEstimate(
            flops=4 * matmuls * length * length * width,
            bytes_accessed=(len(arrays) + outputs) * length * width * 2,
            transcendentals=length * length * width // HEAD_SIZE,
        ),
    )(*arrays, doc_block[:, None], doc_block[None, :])


MESH = pl.DeviceIdType.MESH
LANES = 128


def dot(a, b, ca, cb):
    return lax.dot_general(
        a, b, (((ca,), (cb,)), ((), ())), preferred_element_type=jnp.float32
    )


def line_kernel(
    n,
    levels,
    q_hbm,
    k_hbm,
    v_hbm,
    res_hbm,
    g_hbm,
    w_hbm,
    mom_hbm,
    doc_ref,
    step_ref,
    out_hbm,
    dq_hbm,
    dk_hbm,
    dv_hbm,
    nw_hbm,
    nm_hbm,
    wbuf,
    gown,
    gpair,
    qb,
    kb,
    vb,
    ctx,
    ctxp,
    cg,
    cgs,
    acc,
    oacc,
    osend,
    ogot,
    rs,
    mb,
    st,
    pr,
    rb,
    bias,
    hs,
    ws,
    gs,
    ms,
    ys,
    ns,
    xg_s,
    xg_r,
    xc_s,
    xc_r,
    xb_s,
    xb_r,
    xo_s,
    xo_r,
    zs,
    zr,
    ps,
    pr_r,
):
    units, chunks, rows, wide = wbuf.shape
    heads, tokens, size = qb.shape
    per = heads // n
    scale = HEAD_SIZE ** (-0.5)
    me = lax.axis_index("fsdp")
    rep = lax.axis_index("rep")
    z = lax.div(me, 2)
    x = lax.rem(me, 2)
    pair = me + 1 - 2 * x
    at_end = (z == 0) | (z == n - 1)

    def partner(level):
        bit = lax.rem(lax.div(rep, 1 << level), 2)
        return rep + (1 << level) - (2 << level) * bit

    def lanes(c, width):
        return pl.ds(pl.multiple_of(c * width, width), width)

    def own_rows(u):
        return pl.ds(pl.multiple_of((2 * u + x) * rows, 16), rows)

    def pair_rows(u):
        return pl.ds(pl.multiple_of((2 * u + 1 - x) * rows, 16), rows)

    def head_rows(h):
        return pl.ds(pl.multiple_of(h * size, size), size)

    def load_head(i, h):
        src = (q_hbm, k_hbm, v_hbm)[i]
        dst = (qb, kb, vb)[i]
        return pltpu.make_async_copy(src.at[:, lanes(h, size)], dst.at[h], hs.at[i, h])

    def store_head(i, h):
        src = (qb, kb, vb)[i]
        dst = (dq_hbm, dk_hbm, dv_hbm)[i]
        return pltpu.make_async_copy(src.at[h], dst.at[:, lanes(h, size)], hs.at[i, h])

    def load_w(c):
        return pltpu.make_async_copy(w_hbm.at[:, lanes(c, wide)], wbuf.at[z, c], ws.at[c])

    def load_g(c):
        return pltpu.make_async_copy(g_hbm.at[:, lanes(c, wide)], gown.at[c], gs.at[c])

    def load_m(c):
        return pltpu.make_async_copy(mom_hbm.at[:, lanes(c, wide)], mb.at[c], ms.at[c])

    def store_m(c):
        return pltpu.make_async_copy(mb.at[c], nm_hbm.at[:, lanes(c, wide)], ms.at[c])

    def load_y(c):
        return pltpu.make_async_copy(res_hbm.at[:, lanes(c, wide)], rb.at[c], ys.at[c])

    def store_y(c):
        return pltpu.make_async_copy(rb.at[c], out_hbm.at[:, lanes(c, wide)], ys.at[c])

    def store_n(c):
        return pltpu.make_async_copy(pr.at[0, c], nw_hbm.at[:, lanes(c, wide)], ns.at[c])

    def to_pair(src, dst, send, recv):
        return pltpu.make_async_remote_copy(
            src_ref=src,
            dst_ref=dst,
            send_sem=send,
            recv_sem=recv,
            device_id={"fsdp": pair},
            device_id_type=MESH,
        )

    def x_grad(c):
        return to_pair(g_hbm.at[:, lanes(c, wide)], gpair.at[c], xg_s.at[c], xg_r.at[c])

    def x_context(u):
        return to_pair(ctx.at[pair_rows(u), :], ctxp.at[u], xc_s.at[u], xc_r.at[u])

    def x_back(u):
        return to_pair(cgs.at[u], cg.at[own_rows(u), :], xb_s.at[u], xb_r.at[u])

    def x_out(c):
        return to_pair(osend.at[c], ogot.at[c], xo_s.at[c], xo_r.at[c])

    def along(d, p, c, src, dst):
        return pltpu.make_async_remote_copy(
            src_ref=src,
            dst_ref=dst,
            send_sem=zs.at[d, p - 1, c],
            recv_sem=zr.at[d, p - 1, c],
            device_id={"fsdp": me + 2 - 4 * d},
            device_id_type=MESH,
        )

    def place(d):
        return z + d * (n - 1 - 2 * z)

    def swap(level, c):
        return pltpu.make_async_remote_copy(
            src_ref=st.at[c],
            dst_ref=pr.at[level, c],
            send_sem=ps.at[level, c],
            recv_sem=pr_r.at[level, c],
            device_id={"rep": partner(level)},
            device_id_type=MESH,
        )

    def block_at(i):
        return jnp.where(2 * z < n, n - 1 - i, i)

    def each(count, body):
        def run(i, carry):
            body(i)
            return carry

        lax.fori_loop(0, count, run, 0)

    def start_loads(i):
        u = block_at(i)

        def one(hh):
            for a in range(3):
                load_head(a, u * per + hh).start()

        each(per, one)

    start_loads(0)

    barrier = pltpu.get_barrier_semaphore()
    pl.semaphore_signal(barrier, inc=1, device_id={"fsdp": pair}, device_id_type=MESH)
    for level in range(levels):
        pl.semaphore_signal(
            barrier, inc=1, device_id={"rep": partner(level)}, device_id_type=MESH
        )

    @pl.when(z > 0)
    def _():
        pl.semaphore_signal(barrier, inc=1, device_id={"fsdp": me - 2}, device_id_type=MESH)

    @pl.when(z < n - 1)
    def _():
        pl.semaphore_signal(barrier, inc=1, device_id={"fsdp": me + 2}, device_id_type=MESH)

    pl.semaphore_wait(barrier, 1 + levels + jnp.where(at_end, 1, 2))

    def first_sends(c):
        def one(d):
            @pl.when(place(d) < n - 1)
            def _():
                along(d, 1, c, w_hbm.at[:, lanes(c, wide)], wbuf.at[z, c]).start()

        each(2, one)

    each(chunks, first_sends)
    x_grad(0).start()
    each(n - 1, lambda i: start_loads(i + 1))

    def other_loads(c):
        load_g(c).start()
        load_w(c).start()
        load_m(c).start()
        load_y(c).start()

    each(chunks, other_loads)

    row_ids = jnp.broadcast_to(doc_ref[...], (tokens, tokens))
    column_ids = jnp.transpose(row_ids)
    r = lax.broadcasted_iota(jnp.int32, (tokens, tokens), 0)
    s = lax.broadcasted_iota(jnp.int32, (tokens, tokens), 1)
    bias[...] = jnp.where((s <= r) & (row_ids == column_ids), 0.0, -jnp.inf)

    blocks = tokens // LANES

    def probabilities_of(q, k, i):
        seen = (i + 1) * LANES
        scores = dot(q[i * LANES : seen], k[:seen], 1, 1) * scale
        scores = scores + bias[i * LANES : seen, :seen]
        exponents = jnp.exp(scores - jnp.max(scores, axis=-1, keepdims=True))
        return exponents * (1.0 / jnp.sum(exponents, axis=-1, keepdims=True))

    def forward_head(h):
        q, k, v = qb[h], kb[h], vb[h]
        parts = []
        for i in range(blocks):
            probs = probabilities_of(q, k, i).astype(jnp.bfloat16)
            parts.append(dot(probs, v[: (i + 1) * LANES], 1, 0))
        context = jnp.concatenate(parts, axis=0)
        ctx[head_rows(h), :] = jnp.transpose(context).astype(jnp.bfloat16)

    def forward_block(i):
        u = block_at(i)

        def one(hh):
            h = u * per + hh
            for a in range(3):
                load_head(a, h).wait()
            forward_head(h)

        each(per, one)
        x_context(u).start()

        @pl.when(i == 0)
        def _():
            each(chunks - 1, lambda c: x_grad(c + 1).start())

    each(n, forward_block)

    def wait_loads(c):
        load_g(c).wait()
        load_w(c).wait()
        load_m(c).wait()
        load_y(c).wait()

    each(chunks, wait_loads)

    def backward_head(h):
        q, k, v = qb[h], kb[h], vb[h]
        grad = jnp.transpose(cg[head_rows(h), :].astype(jnp.float32)).astype(jnp.bfloat16)
        low, score_grads, parts = [], [], []
        for i in range(blocks):
            seen = (i + 1) * LANES
            probs = probabilities_of(q, k, i)
            low.append(probs.astype(jnp.bfloat16))
            prob_grad = dot(grad[i * LANES : seen], v[:seen], 1, 1)
            row_delta = jnp.sum(prob_grad * probs, axis=-1, keepdims=True)
            score_grad = (probs * (prob_grad - row_delta) * scale).astype(jnp.bfloat16)
            score_grads.append(score_grad)
            parts.append(dot(score_grad, k[:seen], 1, 0))
        for i in range(blocks):
            cut = slice(i * LANES, (i + 1) * LANES)
            qb[h, cut, :] = parts[i].astype(jnp.bfloat16)
        for j in range(blocks):
            cut = slice(j * LANES, (j + 1) * LANES)
            scores_j = jnp.concatenate([b[:, cut] for b in score_grads[j:]], axis=0)
            probs_j = jnp.concatenate([b[:, cut] for b in low[j:]], axis=0)
            kb[h, cut, :] = dot(scores_j, q[j * LANES :], 0, 0).astype(jnp.bfloat16)
            vb[h, cut, :] = dot(probs_j, grad[j * LANES :], 0, 0).astype(jnp.bfloat16)

    def backward_unit(u):
        x_back(u).wait_recv()

        def one(hh):
            h = u * per + hh
            backward_head(h)
            for a in range(3):
                store_head(a, h).start()

        each(per, one)

    def weight_part(u, c):
        return dot(ctx[own_rows(u), :], gown[c], 1, 0) + dot(ctxp[u], gpair[c], 1, 0)

    def unit_chunk(u, c):
        weight = wbuf[u, c]
        for side in range(2):
            left = ctx[own_rows(u), :] if side == 0 else ctxp[u]
            grad = gown[c] if side == 0 else gpair[c]
            before = jnp.where(u == z, 0.0, oacc[side, c])
            oacc[side, c] = before + dot(left, weight, 0, 0)
            before = jnp.where(c == 0, 0.0, acc[side])
            acc[side] = before + dot(weight, grad, 1, 1)

        @pl.when(c == chunks - 1)
        def _():
            cgs[u] = acc[1].astype(jnp.bfloat16)
            cg[own_rows(u), :] = acc[0].astype(jnp.bfloat16)
            x_back(u).start()

    far = jnp.where(2 * z < n, z + 2, z - 2)

    def finish(c):
        total = weight_part(z, c)
        total = total + jnp.where(z > 0, rs[z, c].astype(jnp.float32), 0.0)
        total = total + jnp.where(z < n - 1, rs[n, c].astype(jnp.float32), 0.0)
        moment = momentum_decay * mb[c] + total
        mb[c] = moment
        stepped = wbuf[z, c].astype(jnp.float32) - learning_rate * moment
        st[c] = stepped.astype(jnp.bfloat16)
        store_m(c).start()
        for level in range(levels):
            swap(level, c).start()
        x_out(c).wait_recv()
        total_out = rb[c].astype(jnp.float32) + oacc[0, c] + ogot[c].astype(jnp.float32)
        rb[c] = total_out.astype(jnp.bfloat16)
        store_y(c).start()

    def average(c):
        for level in range(levels):
            swap(level, c).wait_recv()
        level_now = jnp.full((rows, wide), lax.rem(step_ref[0], levels), jnp.int32)
        other = pr[levels - 1, c].astype(jnp.float32)
        for level in range(levels - 1):
            other = jnp.where(level_now == level, pr[level, c].astype(jnp.float32), other)
        mean = (st[c].astype(jnp.float32) + other) * 0.5
        pr[0, c] = mean.astype(jnp.bfloat16)
        store_n(c).start()

    def step(t):
        p = 2 + lax.div(t, chunks)
        c = lax.rem(t, chunks)

        @pl.when(p <= n + 1)
        def _():
            def arrived(d):
                @pl.when(place(d) > 0)
                def _():
                    along(d, p - 1, c, rs.at[0, 0], rs.at[0, 0]).wait_recv()

            each(2, arrived)

        @pl.when(p <= n)
        def _():
            def forward(d):
                zz = place(d)

                @pl.when((zz < n - 1) & (p <= zz + 1))
                def _():
                    u = zz + 1 - p
                    u = u + d * (n - 1 - 2 * u)
                    along(d, p, c, wbuf.at[u, c], wbuf.at[u, c]).start()

            each(2, forward)

            @pl.when(p == 2)
            def _():
                x_grad(c).wait_recv()

                @pl.when(c == 0)
                def _():
                    x_context(block_at(0)).wait_recv()

            @pl.when((p == 3) & (c == 0))
            def _():
                each(n - 1, lambda i: x_context(block_at(i + 1)).wait_recv())

            def reduce(d):
                zz = place(d)

                @pl.when((zz < n - 1) & (p > zz + 1))
                def _():
                    b = zz + 1 + n - p
                    b = b + d * (n - 1 - 2 * b)
                    before = jnp.where(zz > 0, rs[b, c].astype(jnp.float32), 0.0)
                    rs[b, c] = (before + weight_part(b, c)).astype(jnp.bfloat16)
                    slot = jnp.where((p == n) & (d == 1), n, b)
                    along(d, p, c, rs.at[b, c], rs.at[slot, c]).start()

            each(2, reduce)

        @pl.when(p == n + 1)
        def _():
            finish(c)

        @pl.when(t >= (n - 1) * chunks + 1)
        def _():
            average(t - ((n - 1) * chunks + 1))

        @pl.when((p == 3) | (p == 4))
        def _():
            def unit(i):
                whole = jnp.where(
                    p == 3,
                    jnp.where(c == 0, z, jnp.where(c == 1, z - 1, jnp.where(c == 2, z + 1, -1))),
                    jnp.where(c == 0, far, -1),
                )
                single = jnp.where((p == n) & at_end, n - 1 - z, -1)
                u = jnp.where(i == 0, whole, single)
                low = jnp.where(i == 0, 0, c)
                high = jnp.where(i == 0, chunks, c + 1)

                @pl.when((u >= 0) & (u < n))
                def _():
                    def one(cc, carry):
                        unit_chunk(u, cc)
                        return carry

                    lax.fori_loop(low, high, one, 0)

            each(2, unit)

        @pl.when(p == n)
        def _():
            osend[c] = oacc[1, c].astype(jnp.bfloat16)
            x_out(c).start()

        last = jnp.where(at_end, n - 1 - z, -1)
        back = jnp.where(
            p == 4,
            jnp.where(c == 1, z, jnp.where(c == 2, z - 1, jnp.where(c == 3, z + 1, -1))),
            jnp.where(p == 5, jnp.where(c == 0, far, jnp.where(c == chunks - 2, last, -1)), -1),
        )

        @pl.when((back >= 0) & (back < n))
        def _():
            backward_unit(back)

    each(n * chunks + 1, step)

    def ends(c):
        def line(d):
            @pl.when(place(d) < n - 1)
            def _():
                for p in range(1, n + 1):
                    along(d, p, c, rs.at[0, 0], rs.at[0, 0]).wait_send()

        each(2, line)
        x_grad(c).wait_send()
        x_out(c).wait_send()
        for level in range(levels):
            swap(level, c).wait_send()
        store_m(c).wait()
        store_y(c).wait()
        store_n(c).wait()

    each(chunks, ends)

    def unit_ends(u):
        x_context(u).wait_send()
        x_back(u).wait_send()

    each(n, unit_ends)

    def head_ends(h):
        for a in range(3):
            store_head(a, h).wait()

    each(heads, head_ends)


def line_shape(count, levels, tokens, features, rows, columns):
    n = count // 2
    heads = features // HEAD_SIZE
    wide = 4 * LANES
    fits = (
        count % 2 == 0
        and n == 4
        and levels >= 1
        and tokens % LANES == 0
        and rows % 16 == 0
        and heads % n == 0
        and 2 * rows * n == features
        and columns % wide == 0
        and columns // wide >= 5
    )
    return (n, wide) if fits else None


def on_line(
    n, wide, query, key, value, residual, out_grad, doc_ids, weight, momentum, step_index
):
    tokens, features = query.shape
    rows, columns = weight.shape
    chunks = columns // wide
    heads = features // HEAD_SIZE
    levels = lax.axis_size("rep").bit_length() - 1
    any_space = pl.BlockSpec(memory_space=pl.ANY)
    low, full = jnp.bfloat16, jnp.float32
    dma = pltpu.SemaphoreType.DMA
    like = lambda a: jax.ShapeDtypeStruct(a.shape, a.dtype)
    return pl.pallas_call(
        functools.partial(line_kernel, n, levels),
        in_specs=[any_space] * 7
        + [pl.BlockSpec(memory_space=pltpu.VMEM), pl.BlockSpec(memory_space=pltpu.SMEM)],
        out_specs=[any_space] * 6,
        out_shape=[like(a) for a in (residual, query, key, value, weight, momentum)],
        scratch_shapes=[
            pltpu.VMEM((n, chunks, rows, wide), low),
            pltpu.VMEM((chunks, tokens, wide), low),
            pltpu.VMEM((chunks, tokens, wide), low),
            pltpu.VMEM((heads, tokens, HEAD_SIZE), low),
            pltpu.VMEM((heads, tokens, HEAD_SIZE), low),
            pltpu.VMEM((heads, tokens, HEAD_SIZE), low),
            pltpu.VMEM((features, tokens), low),
            pltpu.VMEM((n, rows, tokens), low),
            pltpu.VMEM((features, tokens), low),
            pltpu.VMEM((n, rows, tokens), low),
            pltpu.VMEM((2, rows, tokens), full),
            pltpu.VMEM((2, chunks, tokens, wide), full),
            pltpu.VMEM((chunks, tokens, wide), low),
            pltpu.VMEM((chunks, tokens, wide), low),
            pltpu.VMEM((n + 1, chunks, rows, wide), low),
            pltpu.VMEM((chunks, rows, wide), full),
            pltpu.VMEM((chunks, rows, wide), low),
            pltpu.VMEM((levels, chunks, rows, wide), low),
            pltpu.VMEM((chunks, tokens, wide), low),
            pltpu.VMEM((tokens, tokens), full),
            dma((3, heads)),
            dma((chunks,)),
            dma((chunks,)),
            dma((chunks,)),
            dma((chunks,)),
            dma((chunks,)),
            dma((chunks,)),
            dma((chunks,)),
            dma((n,)),
            dma((n,)),
            dma((n,)),
            dma((n,)),
            dma((chunks,)),
            dma((chunks,)),
            dma((2, n, chunks)),
            dma((2, n, chunks)),
            dma((levels, chunks)),
            dma((levels, chunks)),
        ],
        compiler_params=pltpu.CompilerParams(
            collective_id=0, has_side_effects=True, vmem_limit_bytes=67043328
        ),
    )(
        query,
        key,
        value,
        residual,
        out_grad,
        weight,
        momentum,
        doc_ids,
        step_index,
    )


def on_device(
    query_rows,
    key_rows,
    value_rows,
    residual_in,
    out_grad,
    doc_ids,
    out_weight,
    momentum,
    step_index,
):
    count = lax.axis_size("fsdp")
    shape = line_shape(
        count,
        lax.axis_size("rep").bit_length() - 1,
        query_rows.shape[1],
        query_rows.shape[2],
        out_weight.shape[1],
        out_weight.shape[2],
    )
    if shape is not None:
        arrays = (query_rows, key_rows, value_rows, residual_in, out_grad)
        results = on_line(
            *shape, *[a[0] for a in arrays], doc_ids, out_weight[0], momentum[0], step_index
        )
        return tuple(r[None] for r in results)
    side = lax.axis_index("fsdp") % 2
    groups = [[i for i in range(count) if i % 2 == s] for s in range(2)]
    pair = [(i, i ^ 1) for i in range(count)]
    first = side == 0
    query, key, value = query_rows[0], key_rows[0], value_rows[0]
    weight_shard = out_weight[0]
    own_grad = out_grad[0]
    rows = weight_shard.shape[0]
    gathered = lax.all_gather(
        weight_shard, "fsdp", axis=0, tiled=True, axis_index_groups=groups
    )
    pair_grad = lax.ppermute(own_grad, "fsdp", pair)
    (context,) = per_head(forward_kernel, (query, key, value), doc_ids[0], 1, 2)

    def half(array, which):
        return jnp.concatenate(
            [array[:, j * rows : (j + 1) * rows] for j in range(which, count, 2)], axis=1
        )

    low, high = half(context, 0), half(context, 1)
    own_context = jnp.where(first, low, high)
    pair_context = lax.ppermute(jnp.where(first, high, low), "fsdp", pair)

    def outer(left, right):
        return lax.dot_general(
            left, right, (((0,), (0,)), ((), ())), preferred_element_type=jnp.float32
        )

    weight_term = (outer(own_context, own_grad) + outer(pair_context, pair_grad)).astype(
        jnp.bfloat16
    )
    weight_grad = lax.psum_scatter(
        weight_term, "fsdp", scatter_dimension=0, tiled=True, axis_index_groups=groups
    ).astype(jnp.float32)

    def back(grad):
        return lax.dot_general(
            grad, gathered, (((1,), (1,)), ((), ())), preferred_element_type=jnp.float32
        ).astype(jnp.bfloat16)

    got_back = lax.ppermute(back(pair_grad), "fsdp", pair)
    pair_out = jnp.dot(pair_context, gathered, preferred_element_type=jnp.float32)
    got_out = lax.ppermute(pair_out.astype(jnp.bfloat16), "fsdp", pair)
    own_back = back(own_grad)
    even = jnp.where(first, own_back, got_back)
    odd = jnp.where(first, got_back, own_back)
    pieces = []
    for j in range(count // 2):
        cut = slice(j * rows, (j + 1) * rows)
        pieces += [even[:, cut], odd[:, cut]]
    context_grad = jnp.concatenate(pieces, axis=1)
    query_grad, key_grad, value_grad = per_head(
        backward_kernel, (query, key, value, context_grad), doc_ids[0], 3, 5
    )
    own_out = jnp.dot(own_context, gathered, preferred_element_type=jnp.float32)
    block_out = (
        residual_in[0].astype(jnp.float32) + own_out + got_out.astype(jnp.float32)
    ).astype(jnp.bfloat16)

    new_momentum = momentum_decay * momentum[0] + weight_grad
    stepped = (weight_shard.astype(jnp.float32) - learning_rate * new_momentum).astype(jnp.bfloat16)
    levels = lax.axis_size("rep").bit_length() - 1
    branches = [functools.partial(swapped, axis="rep", distance=level) for level in range(levels)]
    partner = lax.switch(step_index[0] % levels, branches, stepped)
    new_weight = ((stepped.astype(jnp.float32) + partner.astype(jnp.float32)) * 0.5).astype(
        jnp.bfloat16
    )
    return (
        block_out[None],
        query_grad[None],
        key_grad[None],
        value_grad[None],
        new_weight[None],
        new_momentum[None],
    )


def solution(mesh):
    rows = P("rep", "fsdp", None)
    return jax.shard_map(
        on_device,
        mesh=mesh,
        in_specs=(rows, rows, rows, rows, rows, P("rep", "fsdp"), rows, rows, P()),
        out_specs=(rows,) * 6,
        check_vma=False,
    )
```

```python
import functools

import jax
import jax.numpy as jnp
from jax import lax
from jax.experimental import pallas as pl
from jax.experimental.pallas import tpu as pltpu
from jax.sharding import PartitionSpec as P

HEAD_SIZE = 128

momentum_decay = 0.9
learning_rate = 0.0003


def swapped(block, axis, distance):
    count = lax.axis_size(axis)
    route = []
    for low in range(count):
        high = low | 1 << distance
        if high != low and high < count:
            route += [(low, high), (high, low)]
    return lax.ppermute(block, axis, route)


def probabilities(q, k, doc_column, doc_row):
    length = q.shape[0]
    scores = lax.dot_general(
        q, k, (((1,), (1,)), ((), ())), preferred_element_type=jnp.float32
    ) * (HEAD_SIZE ** (-0.5))
    rows = lax.broadcasted_iota(jnp.int32, (length, length), 0)
    columns = lax.broadcasted_iota(jnp.int32, (length, length), 1)
    allowed = (columns <= rows) & (doc_column == doc_row)
    scores = jnp.where(allowed, scores, -jnp.inf)
    exponents = jnp.exp(scores - jnp.max(scores, axis=-1, keepdims=True))
    return exponents / jnp.sum(exponents, axis=-1, keepdims=True)


def forward_kernel(q_ref, k_ref, v_ref, doc_column_ref, doc_row_ref, context_ref):
    for head in range(q_ref.shape[1] // HEAD_SIZE):
        cut = slice(head * HEAD_SIZE, (head + 1) * HEAD_SIZE)
        probs = probabilities(q_ref[:, cut], k_ref[:, cut], doc_column_ref[...], doc_row_ref[...])
        context_ref[:, cut] = jnp.dot(
            probs.astype(jnp.bfloat16), v_ref[:, cut], preferred_element_type=jnp.float32
        ).astype(jnp.bfloat16)


def backward_kernel(
    q_ref, k_ref, v_ref, grad_ref, doc_column_ref, doc_row_ref, dq_ref, dk_ref, dv_ref
):
    for head in range(q_ref.shape[1] // HEAD_SIZE):
        cut = slice(head * HEAD_SIZE, (head + 1) * HEAD_SIZE)
        q, k, v, grad = q_ref[:, cut], k_ref[:, cut], v_ref[:, cut], grad_ref[:, cut]
        probs = probabilities(q, k, doc_column_ref[...], doc_row_ref[...])
        dv_ref[:, cut] = lax.dot_general(
            probs.astype(jnp.bfloat16),
            grad,
            (((0,), (0,)), ((), ())),
            preferred_element_type=jnp.float32,
        ).astype(jnp.bfloat16)
        prob_grad = lax.dot_general(
            grad, v, (((1,), (1,)), ((), ())), preferred_element_type=jnp.float32
        )
        row_delta = jnp.sum(prob_grad * probs, axis=-1, keepdims=True)
        score_grad = (probs * (prob_grad - row_delta) * (HEAD_SIZE ** (-0.5))).astype(jnp.bfloat16)
        dq_ref[:, cut] = jnp.dot(score_grad, k, preferred_element_type=jnp.float32).astype(
            jnp.bfloat16
        )
        dk_ref[:, cut] = lax.dot_general(
            score_grad, q, (((0,), (0,)), ((), ())), preferred_element_type=jnp.float32
        ).astype(jnp.bfloat16)


def per_head(kernel, arrays, doc_block, outputs, matmuls):
    length, width = arrays[0].shape
    step = 2 * HEAD_SIZE if width % (2 * HEAD_SIZE) == 0 else HEAD_SIZE
    block = pl.BlockSpec((length, step), lambda h: (0, h))
    whole = lambda shape: pl.BlockSpec(shape, lambda h: (0, 0))
    result = jax.ShapeDtypeStruct((length, width), jnp.bfloat16)
    return pl.pallas_call(
        kernel,
        grid=(width // step,),
        in_specs=[block] * len(arrays) + [whole((length, 1)), whole((1, length))],
        out_specs=[block] * outputs,
        out_shape=[result] * outputs,
        cost_estimate=pl.CostEstimate(
            flops=4 * matmuls * length * length * width,
            bytes_accessed=(len(arrays) + outputs) * length * width * 2,
            transcendentals=length * length * width // HEAD_SIZE,
        ),
    )(*arrays, doc_block[:, None], doc_block[None, :])


MESH = pl.DeviceIdType.MESH
LANES = 128


def dot(a, b, ca, cb):
    return lax.dot_general(
        a, b, (((ca,), (cb,)), ((), ())), preferred_element_type=jnp.float32
    )


def line_kernel(
    n,
    levels,
    q_hbm,
    k_hbm,
    v_hbm,
    res_hbm,
    g_hbm,
    w_hbm,
    mom_hbm,
    doc_ref,
    step_ref,
    rb,
    qb,
    kb,
    vb,
    nb,
    mb,
    wbuf,
    gown,
    gpair,
    ctx,
    ctxp,
    cg,
    cgs,
    acc,
    oacc,
    osend,
    ogot,
    rs,
    st,
    pr,
    bias,
    hs,
    ws,
    gs,
    ms,
    ys,
    xg_s,
    xg_r,
    xc_s,
    xc_r,
    xb_s,
    xb_r,
    xo_s,
    xo_r,
    zs,
    zr,
    ps,
    pr_r,
):
    units, chunks, rows, wide = wbuf.shape
    heads, tokens, size = qb.shape
    per = heads // n
    scale = HEAD_SIZE ** (-0.5)
    me = lax.axis_index("fsdp")
    rep = lax.axis_index("rep")
    z = lax.div(me, 2)
    x = lax.rem(me, 2)
    pair = me + 1 - 2 * x
    at_end = (z == 0) | (z == n - 1)

    def partner(level):
        bit = lax.rem(lax.div(rep, 1 << level), 2)
        return rep + (1 << level) - (2 << level) * bit

    def lanes(c, width):
        return pl.ds(pl.multiple_of(c * width, width), width)

    def own_rows(u):
        return pl.ds(pl.multiple_of((2 * u + x) * rows, 16), rows)

    def pair_rows(u):
        return pl.ds(pl.multiple_of((2 * u + 1 - x) * rows, 16), rows)

    def head_rows(h):
        return pl.ds(pl.multiple_of(h * size, size), size)

    def load_head(i, h):
        src = (q_hbm, k_hbm, v_hbm)[i]
        dst = (qb, kb, vb)[i]
        return pltpu.make_async_copy(src.at[:, lanes(h, size)], dst.at[h], hs.at[i, h])

    def load_w(c):
        return pltpu.make_async_copy(w_hbm.at[:, lanes(c, wide)], wbuf.at[z, c], ws.at[c])

    def load_g(c):
        return pltpu.make_async_copy(g_hbm.at[:, lanes(c, wide)], gown.at[c], gs.at[c])

    def load_m(c):
        return pltpu.make_async_copy(mom_hbm.at[:, lanes(c, wide)], mb.at[c], ms.at[c])

    def load_y(c):
        return pltpu.make_async_copy(res_hbm.at[:, lanes(c, wide)], rb.at[c], ys.at[c])

    def to_pair(src, dst, send, recv):
        return pltpu.make_async_remote_copy(
            src_ref=src,
            dst_ref=dst,
            send_sem=send,
            recv_sem=recv,
            device_id={"fsdp": pair},
            device_id_type=MESH,
        )

    def x_grad(c):
        return to_pair(g_hbm.at[:, lanes(c, wide)], gpair.at[c], xg_s.at[c], xg_r.at[c])

    def x_context(u):
        return to_pair(ctx.at[pair_rows(u), :], ctxp.at[u], xc_s.at[u], xc_r.at[u])

    def x_back(u):
        return to_pair(cgs.at[u], cg.at[own_rows(u), :], xb_s.at[u], xb_r.at[u])

    def x_out(c):
        return to_pair(osend.at[c], ogot.at[c], xo_s.at[c], xo_r.at[c])

    def along(d, p, c, src, dst):
        return pltpu.make_async_remote_copy(
            src_ref=src,
            dst_ref=dst,
            send_sem=zs.at[d, p - 1, c],
            recv_sem=zr.at[d, p - 1, c],
            device_id={"fsdp": me + 2 - 4 * d},
            device_id_type=MESH,
        )

    def place(d):
        return z + d * (n - 1 - 2 * z)

    def swap(level, c):
        return pltpu.make_async_remote_copy(
            src_ref=st.at[c],
            dst_ref=pr.at[level, c],
            send_sem=ps.at[level, c],
            recv_sem=pr_r.at[level, c],
            device_id={"rep": partner(level)},
            device_id_type=MESH,
        )

    def block_at(i):
        return jnp.where(2 * z < n, n - 1 - i, i)

    def each(count, body):
        def run(i, carry):
            body(i)
            return carry

        lax.fori_loop(0, count, run, 0)

    def start_loads(i):
        u = block_at(i)

        def one(hh):
            for a in range(3):
                load_head(a, u * per + hh).start()

        each(per, one)

    start_loads(0)

    barrier = pltpu.get_barrier_semaphore()
    pl.semaphore_signal(barrier, inc=1, device_id={"fsdp": pair}, device_id_type=MESH)
    for level in range(levels):
        pl.semaphore_signal(
            barrier, inc=1, device_id={"rep": partner(level)}, device_id_type=MESH
        )

    @pl.when(z > 0)
    def _():
        pl.semaphore_signal(barrier, inc=1, device_id={"fsdp": me - 2}, device_id_type=MESH)

    @pl.when(z < n - 1)
    def _():
        pl.semaphore_signal(barrier, inc=1, device_id={"fsdp": me + 2}, device_id_type=MESH)

    pl.semaphore_wait(barrier, 1 + levels + jnp.where(at_end, 1, 2))

    def first_sends(c):
        def one(d):
            @pl.when(place(d) < n - 1)
            def _():
                along(d, 1, c, w_hbm.at[:, lanes(c, wide)], wbuf.at[z, c]).start()

        each(2, one)

    each(chunks, first_sends)
    x_grad(0).start()
    each(n - 1, lambda i: start_loads(i + 1))

    def other_loads(c):
        load_g(c).start()
        load_w(c).start()
        load_m(c).start()
        load_y(c).start()

    each(chunks, other_loads)

    row_ids = jnp.broadcast_to(doc_ref[...], (tokens, tokens))
    column_ids = jnp.transpose(row_ids)
    r = lax.broadcasted_iota(jnp.int32, (tokens, tokens), 0)
    s = lax.broadcasted_iota(jnp.int32, (tokens, tokens), 1)
    bias[...] = jnp.where((s <= r) & (row_ids == column_ids), 0.0, -jnp.inf)

    blocks = tokens // LANES

    def probabilities_of(q, k, i):
        seen = (i + 1) * LANES
        scores = dot(q[i * LANES : seen], k[:seen], 1, 1) * scale
        scores = scores + bias[i * LANES : seen, :seen]
        exponents = jnp.exp(scores - jnp.max(scores, axis=-1, keepdims=True))
        return exponents * (1.0 / jnp.sum(exponents, axis=-1, keepdims=True))

    def forward_head(h):
        q, k, v = qb[h], kb[h], vb[h]
        parts = []
        for i in range(blocks):
            probs = probabilities_of(q, k, i).astype(jnp.bfloat16)
            parts.append(dot(probs, v[: (i + 1) * LANES], 1, 0))
        context = jnp.concatenate(parts, axis=0)
        ctx[head_rows(h), :] = jnp.transpose(context).astype(jnp.bfloat16)

    def forward_block(i):
        u = block_at(i)

        def one(hh):
            h = u * per + hh
            for a in range(3):
                load_head(a, h).wait()
            forward_head(h)

        each(per, one)
        x_context(u).start()

        @pl.when(i == 0)
        def _():
            each(chunks - 1, lambda c: x_grad(c + 1).start())

    each(n, forward_block)

    def wait_loads(c):
        load_g(c).wait()
        load_w(c).wait()
        load_m(c).wait()
        load_y(c).wait()

    each(chunks, wait_loads)

    def backward_head(h):
        q, k, v = qb[h], kb[h], vb[h]
        grad = jnp.transpose(cg[head_rows(h), :].astype(jnp.float32)).astype(jnp.bfloat16)
        low, score_grads, parts = [], [], []
        for i in range(blocks):
            seen = (i + 1) * LANES
            probs = probabilities_of(q, k, i)
            low.append(probs.astype(jnp.bfloat16))
            prob_grad = dot(grad[i * LANES : seen], v[:seen], 1, 1)
            row_delta = jnp.sum(prob_grad * probs, axis=-1, keepdims=True)
            score_grad = (probs * (prob_grad - row_delta) * scale).astype(jnp.bfloat16)
            score_grads.append(score_grad)
            parts.append(dot(score_grad, k[:seen], 1, 0))
        for i in range(blocks):
            cut = slice(i * LANES, (i + 1) * LANES)
            qb[h, cut, :] = parts[i].astype(jnp.bfloat16)
        for j in range(blocks):
            cut = slice(j * LANES, (j + 1) * LANES)
            scores_j = jnp.concatenate([b[:, cut] for b in score_grads[j:]], axis=0)
            probs_j = jnp.concatenate([b[:, cut] for b in low[j:]], axis=0)
            kb[h, cut, :] = dot(scores_j, q[j * LANES :], 0, 0).astype(jnp.bfloat16)
            vb[h, cut, :] = dot(probs_j, grad[j * LANES :], 0, 0).astype(jnp.bfloat16)

    def backward_unit(u):
        x_back(u).wait_recv()

        def one(hh):
            backward_head(u * per + hh)

        each(per, one)

    def weight_part(u, c):
        return dot(ctx[own_rows(u), :], gown[c], 1, 0) + dot(ctxp[u], gpair[c], 1, 0)

    def unit_chunk(u, c):
        weight = wbuf[u, c]
        for side in range(2):
            left = ctx[own_rows(u), :] if side == 0 else ctxp[u]
            grad = gown[c] if side == 0 else gpair[c]
            before = jnp.where(u == z, 0.0, oacc[side, c])
            oacc[side, c] = before + dot(left, weight, 0, 0)
            before = jnp.where(c == 0, 0.0, acc[side])
            acc[side] = before + dot(weight, grad, 1, 1)

        @pl.when(c == chunks - 1)
        def _():
            cgs[u] = acc[1].astype(jnp.bfloat16)
            cg[own_rows(u), :] = acc[0].astype(jnp.bfloat16)
            x_back(u).start()

    far = jnp.where(2 * z < n, z + 2, z - 2)

    def finish(c):
        total = weight_part(z, c)
        total = total + jnp.where(z > 0, rs[z, c].astype(jnp.float32), 0.0)
        total = total + jnp.where(z < n - 1, rs[n, c].astype(jnp.float32), 0.0)
        moment = momentum_decay * mb[c] + total
        mb[c] = moment
        stepped = wbuf[z, c].astype(jnp.float32) - learning_rate * moment
        st[c] = stepped.astype(jnp.bfloat16)
        for level in range(levels):
            swap(level, c).start()
        x_out(c).wait_recv()
        total_out = rb[c].astype(jnp.float32) + oacc[0, c] + ogot[c].astype(jnp.float32)
        rb[c] = total_out.astype(jnp.bfloat16)

    def average(c):
        for level in range(levels):
            swap(level, c).wait_recv()
        level_now = jnp.full((rows, wide), lax.rem(step_ref[0], levels), jnp.int32)
        other = pr[levels - 1, c].astype(jnp.float32)
        for level in range(levels - 1):
            other = jnp.where(level_now == level, pr[level, c].astype(jnp.float32), other)
        mean = (st[c].astype(jnp.float32) + other) * 0.5
        nb[c] = mean.astype(jnp.bfloat16)

    def step(t):
        p = 2 + lax.div(t, chunks)
        c = lax.rem(t, chunks)

        @pl.when(p <= n + 1)
        def _():
            def arrived(d):
                @pl.when(place(d) > 0)
                def _():
                    along(d, p - 1, c, rs.at[0, 0], rs.at[0, 0]).wait_recv()

            each(2, arrived)

        @pl.when(p <= n)
        def _():
            def forward(d):
                zz = place(d)

                @pl.when((zz < n - 1) & (p <= zz + 1))
                def _():
                    u = zz + 1 - p
                    u = u + d * (n - 1 - 2 * u)
                    along(d, p, c, wbuf.at[u, c], wbuf.at[u, c]).start()

            each(2, forward)

            @pl.when(p == 2)
            def _():
                x_grad(c).wait_recv()

                @pl.when(c == 0)
                def _():
                    x_context(block_at(0)).wait_recv()

            @pl.when((p == 3) & (c == 0))
            def _():
                each(n - 1, lambda i: x_context(block_at(i + 1)).wait_recv())

            def reduce(d):
                zz = place(d)

                @pl.when((zz < n - 1) & (p > zz + 1))
                def _():
                    b = zz + 1 + n - p
                    b = b + d * (n - 1 - 2 * b)
                    before = jnp.where(zz > 0, rs[b, c].astype(jnp.float32), 0.0)
                    rs[b, c] = (before + weight_part(b, c)).astype(jnp.bfloat16)
                    slot = jnp.where((p == n) & (d == 1), n, b)
                    along(d, p, c, rs.at[b, c], rs.at[slot, c]).start()

            each(2, reduce)

        @pl.when(p == n + 1)
        def _():
            finish(c)

        @pl.when(t >= (n - 1) * chunks + 1)
        def _():
            average(t - ((n - 1) * chunks + 1))

        @pl.when((p == 3) | (p == 4))
        def _():
            def unit(i):
                whole = jnp.where(
                    p == 3,
                    jnp.where(c == 0, z, jnp.where(c == 1, z - 1, jnp.where(c == 2, z + 1, -1))),
                    jnp.where(c == 0, far, -1),
                )
                single = jnp.where((p == n) & at_end, n - 1 - z, -1)
                u = jnp.where(i == 0, whole, single)
                low = jnp.where(i == 0, 0, c)
                high = jnp.where(i == 0, chunks, c + 1)

                @pl.when((u >= 0) & (u < n))
                def _():
                    def one(cc, carry):
                        unit_chunk(u, cc)
                        return carry

                    lax.fori_loop(low, high, one, 0)

            each(2, unit)

        @pl.when(p == n)
        def _():
            osend[c] = oacc[1, c].astype(jnp.bfloat16)
            x_out(c).start()

        last = jnp.where(at_end, n - 1 - z, -1)
        back = jnp.where(
            p == 4,
            jnp.where(c == 1, z, jnp.where(c == 2, z - 1, jnp.where(c == 3, z + 1, -1))),
            jnp.where(p == 5, jnp.where(c == 0, far, jnp.where(c == chunks - 2, last, -1)), -1),
        )

        @pl.when((back >= 0) & (back < n))
        def _():
            backward_unit(back)

    each(n * chunks + 1, step)

    def ends(c):
        def line(d):
            @pl.when(place(d) < n - 1)
            def _():
                for p in range(1, n + 1):
                    along(d, p, c, rs.at[0, 0], rs.at[0, 0]).wait_send()

        each(2, line)
        x_grad(c).wait_send()
        x_out(c).wait_send()
        for level in range(levels):
            swap(level, c).wait_send()

    each(chunks, ends)

    def unit_ends(u):
        x_context(u).wait_send()
        x_back(u).wait_send()

    each(n, unit_ends)


def write_kernel(
    rb, qb, kb, vb, nb, mb, out_hbm, dq_hbm, dk_hbm, dv_hbm, nw_hbm, nm_hbm, hs, cs
):
    heads, _, size = qb.shape
    chunks, _, wide = rb.shape

    def head(h):
        lanes = pl.ds(pl.multiple_of(h * size, size), size)
        return [
            pltpu.make_async_copy(src.at[h], dst.at[:, lanes], hs.at[i, h])
            for i, (src, dst) in enumerate(((qb, dq_hbm), (kb, dk_hbm), (vb, dv_hbm)))
        ]

    def chunk(c):
        lanes = pl.ds(pl.multiple_of(c * wide, wide), wide)
        return [
            pltpu.make_async_copy(src.at[c], dst.at[:, lanes], cs.at[i, c])
            for i, (src, dst) in enumerate(((rb, out_hbm), (nb, nw_hbm), (mb, nm_hbm)))
        ]

    def start(count, copies):
        def one(i, carry):
            for copy in copies(i):
                copy.start()
            return carry

        lax.fori_loop(0, count, one, 0)

    def wait(count, copies):
        def one(i, carry):
            for copy in copies(i):
                copy.wait()
            return carry

        lax.fori_loop(0, count, one, 0)

    start(chunks, chunk)
    start(heads, head)
    wait(chunks, chunk)
    wait(heads, head)


def line_shape(count, levels, tokens, features, rows, columns):
    n = count // 2
    heads = features // HEAD_SIZE
    wide = 4 * LANES
    fits = (
        count % 2 == 0
        and n == 4
        and levels >= 1
        and tokens % LANES == 0
        and rows % 16 == 0
        and heads % n == 0
        and 2 * rows * n == features
        and columns % wide == 0
        and columns // wide >= 5
    )
    return (n, wide) if fits else None


def on_line(
    n, wide, query, key, value, residual, out_grad, doc_ids, weight, momentum, step_index
):
    tokens, features = query.shape
    rows, columns = weight.shape
    chunks = columns // wide
    heads = features // HEAD_SIZE
    levels = lax.axis_size("rep").bit_length() - 1
    any_space = pl.BlockSpec(memory_space=pl.ANY)
    in_vmem = pl.BlockSpec(memory_space=pltpu.VMEM)
    low, full = jnp.bfloat16, jnp.float32
    dma = pltpu.SemaphoreType.DMA
    like = lambda a: jax.ShapeDtypeStruct(a.shape, a.dtype)
    by_head = pltpu.VMEM((heads, tokens, HEAD_SIZE), low)
    held = pl.pallas_call(
        functools.partial(line_kernel, n, levels),
        in_specs=[any_space] * 7 + [in_vmem, pl.BlockSpec(memory_space=pltpu.SMEM)],
        out_specs=[in_vmem] * 6,
        out_shape=[
            pltpu.VMEM((chunks, tokens, wide), low),
            by_head,
            by_head,
            by_head,
            pltpu.VMEM((chunks, rows, wide), low),
            pltpu.VMEM((chunks, rows, wide), full),
        ],
        scratch_shapes=[
            pltpu.VMEM((n, chunks, rows, wide), low),
            pltpu.VMEM((chunks, tokens, wide), low),
            pltpu.VMEM((chunks, tokens, wide), low),
            pltpu.VMEM((features, tokens), low),
            pltpu.VMEM((n, rows, tokens), low),
            pltpu.VMEM((features, tokens), low),
            pltpu.VMEM((n, rows, tokens), low),
            pltpu.VMEM((2, rows, tokens), full),
            pltpu.VMEM((2, chunks, tokens, wide), full),
            pltpu.VMEM((chunks, tokens, wide), low),
            pltpu.VMEM((chunks, tokens, wide), low),
            pltpu.VMEM((n + 1, chunks, rows, wide), low),
            pltpu.VMEM((chunks, rows, wide), low),
            pltpu.VMEM((levels, chunks, rows, wide), low),
            pltpu.VMEM((tokens, tokens), full),
            dma((3, heads)),
            dma((chunks,)),
            dma((chunks,)),
            dma((chunks,)),
            dma((chunks,)),
            dma((chunks,)),
            dma((chunks,)),
            dma((n,)),
            dma((n,)),
            dma((n,)),
            dma((n,)),
            dma((chunks,)),
            dma((chunks,)),
            dma((2, n, chunks)),
            dma((2, n, chunks)),
            dma((levels, chunks)),
            dma((levels, chunks)),
        ],
        compiler_params=pltpu.CompilerParams(
            collective_id=0, has_side_effects=True, vmem_limit_bytes=50 << 20
        ),
    )(
        query,
        key,
        value,
        residual,
        out_grad,
        weight,
        momentum,
        doc_ids,
        step_index,
    )
    return pl.pallas_call(
        write_kernel,
        in_specs=[any_space] * 6,
        out_specs=[any_space] * 6,
        out_shape=[like(a) for a in (residual, query, key, value, weight, momentum)],
        scratch_shapes=[dma((3, heads)), dma((3, chunks))],
        compiler_params=pltpu.CompilerParams(vmem_limit_bytes=1 << 20),
    )(*held)


def on_device(
    query_rows,
    key_rows,
    value_rows,
    residual_in,
    out_grad,
    doc_ids,
    out_weight,
    momentum,
    step_index,
):
    count = lax.axis_size("fsdp")
    shape = line_shape(
        count,
        lax.axis_size("rep").bit_length() - 1,
        query_rows.shape[1],
        query_rows.shape[2],
        out_weight.shape[1],
        out_weight.shape[2],
    )
    if shape is not None:
        arrays = (query_rows, key_rows, value_rows, residual_in, out_grad)
        results = on_line(
            *shape, *[a[0] for a in arrays], doc_ids, out_weight[0], momentum[0], step_index
        )
        return tuple(r[None] for r in results)
    side = lax.axis_index("fsdp") % 2
    groups = [[i for i in range(count) if i % 2 == s] for s in range(2)]
    pair = [(i, i ^ 1) for i in range(count)]
    first = side == 0
    query, key, value = query_rows[0], key_rows[0], value_rows[0]
    weight_shard = out_weight[0]
    own_grad = out_grad[0]
    rows = weight_shard.shape[0]
    gathered = lax.all_gather(
        weight_shard, "fsdp", axis=0, tiled=True, axis_index_groups=groups
    )
    pair_grad = lax.ppermute(own_grad, "fsdp", pair)
    (context,) = per_head(forward_kernel, (query, key, value), doc_ids[0], 1, 2)

    def half(array, which):
        return jnp.concatenate(
            [array[:, j * rows : (j + 1) * rows] for j in range(which, count, 2)], axis=1
        )

    low, high = half(context, 0), half(context, 1)
    own_context = jnp.where(first, low, high)
    pair_context = lax.ppermute(jnp.where(first, high, low), "fsdp", pair)

    def outer(left, right):
        return lax.dot_general(
            left, right, (((0,), (0,)), ((), ())), preferred_element_type=jnp.float32
        )

    weight_term = (outer(own_context, own_grad) + outer(pair_context, pair_grad)).astype(
        jnp.bfloat16
    )
    weight_grad = lax.psum_scatter(
        weight_term, "fsdp", scatter_dimension=0, tiled=True, axis_index_groups=groups
    ).astype(jnp.float32)

    def back(grad):
        return lax.dot_general(
            grad, gathered, (((1,), (1,)), ((), ())), preferred_element_type=jnp.float32
        ).astype(jnp.bfloat16)

    got_back = lax.ppermute(back(pair_grad), "fsdp", pair)
    pair_out = jnp.dot(pair_context, gathered, preferred_element_type=jnp.float32)
    got_out = lax.ppermute(pair_out.astype(jnp.bfloat16), "fsdp", pair)
    own_back = back(own_grad)
    even = jnp.where(first, own_back, got_back)
    odd = jnp.where(first, got_back, own_back)
    pieces = []
    for j in range(count // 2):
        cut = slice(j * rows, (j + 1) * rows)
        pieces += [even[:, cut], odd[:, cut]]
    context_grad = jnp.concatenate(pieces, axis=1)
    query_grad, key_grad, value_grad = per_head(
        backward_kernel, (query, key, value, context_grad), doc_ids[0], 3, 5
    )
    own_out = jnp.dot(own_context, gathered, preferred_element_type=jnp.float32)
    block_out = (
        residual_in[0].astype(jnp.float32) + own_out + got_out.astype(jnp.float32)
    ).astype(jnp.bfloat16)

    new_momentum = momentum_decay * momentum[0] + weight_grad
    stepped = (weight_shard.astype(jnp.float32) - learning_rate * new_momentum).astype(jnp.bfloat16)
    levels = lax.axis_size("rep").bit_length() - 1
    branches = [functools.partial(swapped, axis="rep", distance=level) for level in range(levels)]
    partner = lax.switch(step_index[0] % levels, branches, stepped)
    new_weight = ((stepped.astype(jnp.float32) + partner.astype(jnp.float32)) * 0.5).astype(
        jnp.bfloat16
    )
    return (
        block_out[None],
        query_grad[None],
        key_grad[None],
        value_grad[None],
        new_weight[None],
        new_momentum[None],
    )


def solution(mesh):
    rows = P("rep", "fsdp", None)
    return jax.shard_map(
        on_device,
        mesh=mesh,
        in_specs=(rows, rows, rows, rows, rows, P("rep", "fsdp"), rows, rows, P()),
        out_specs=(rows,) * 6,
        check_vma=False,
    )
```

```python
import functools

import jax
import jax.numpy as jnp
from jax import lax
from jax.experimental import pallas as pl
from jax.experimental.pallas import tpu as pltpu
from jax.sharding import PartitionSpec as P

HEAD_SIZE = 128

momentum_decay = 0.9
learning_rate = 0.0003


def swapped(block, axis, distance):
    count = lax.axis_size(axis)
    route = []
    for low in range(count):
        high = low | 1 << distance
        if high != low and high < count:
            route += [(low, high), (high, low)]
    return lax.ppermute(block, axis, route)


def probabilities(q, k, doc_column, doc_row):
    length = q.shape[0]
    scores = lax.dot_general(
        q, k, (((1,), (1,)), ((), ())), preferred_element_type=jnp.float32
    ) * (HEAD_SIZE ** (-0.5))
    rows = lax.broadcasted_iota(jnp.int32, (length, length), 0)
    columns = lax.broadcasted_iota(jnp.int32, (length, length), 1)
    allowed = (columns <= rows) & (doc_column == doc_row)
    scores = jnp.where(allowed, scores, -jnp.inf)
    exponents = jnp.exp(scores - jnp.max(scores, axis=-1, keepdims=True))
    return exponents / jnp.sum(exponents, axis=-1, keepdims=True)


def forward_kernel(q_ref, k_ref, v_ref, doc_column_ref, doc_row_ref, context_ref):
    for head in range(q_ref.shape[1] // HEAD_SIZE):
        cut = slice(head * HEAD_SIZE, (head + 1) * HEAD_SIZE)
        probs = probabilities(q_ref[:, cut], k_ref[:, cut], doc_column_ref[...], doc_row_ref[...])
        context_ref[:, cut] = jnp.dot(
            probs.astype(jnp.bfloat16), v_ref[:, cut], preferred_element_type=jnp.float32
        ).astype(jnp.bfloat16)


def backward_kernel(
    q_ref, k_ref, v_ref, grad_ref, doc_column_ref, doc_row_ref, dq_ref, dk_ref, dv_ref
):
    for head in range(q_ref.shape[1] // HEAD_SIZE):
        cut = slice(head * HEAD_SIZE, (head + 1) * HEAD_SIZE)
        q, k, v, grad = q_ref[:, cut], k_ref[:, cut], v_ref[:, cut], grad_ref[:, cut]
        probs = probabilities(q, k, doc_column_ref[...], doc_row_ref[...])
        dv_ref[:, cut] = lax.dot_general(
            probs.astype(jnp.bfloat16),
            grad,
            (((0,), (0,)), ((), ())),
            preferred_element_type=jnp.float32,
        ).astype(jnp.bfloat16)
        prob_grad = lax.dot_general(
            grad, v, (((1,), (1,)), ((), ())), preferred_element_type=jnp.float32
        )
        row_delta = jnp.sum(prob_grad * probs, axis=-1, keepdims=True)
        score_grad = (probs * (prob_grad - row_delta) * (HEAD_SIZE ** (-0.5))).astype(jnp.bfloat16)
        dq_ref[:, cut] = jnp.dot(score_grad, k, preferred_element_type=jnp.float32).astype(
            jnp.bfloat16
        )
        dk_ref[:, cut] = lax.dot_general(
            score_grad, q, (((0,), (0,)), ((), ())), preferred_element_type=jnp.float32
        ).astype(jnp.bfloat16)


def per_head(kernel, arrays, doc_block, outputs, matmuls):
    length, width = arrays[0].shape
    step = 2 * HEAD_SIZE if width % (2 * HEAD_SIZE) == 0 else HEAD_SIZE
    block = pl.BlockSpec((length, step), lambda h: (0, h))
    whole = lambda shape: pl.BlockSpec(shape, lambda h: (0, 0))
    result = jax.ShapeDtypeStruct((length, width), jnp.bfloat16)
    return pl.pallas_call(
        kernel,
        grid=(width // step,),
        in_specs=[block] * len(arrays) + [whole((length, 1)), whole((1, length))],
        out_specs=[block] * outputs,
        out_shape=[result] * outputs,
        cost_estimate=pl.CostEstimate(
            flops=4 * matmuls * length * length * width,
            bytes_accessed=(len(arrays) + outputs) * length * width * 2,
            transcendentals=length * length * width // HEAD_SIZE,
        ),
    )(*arrays, doc_block[:, None], doc_block[None, :])


MESH = pl.DeviceIdType.MESH
LANES = 128
COARSE, FINE = 2, 2


def dot(a, b, ca, cb):
    return lax.dot_general(
        a, b, (((ca,), (cb,)), ((), ())), preferred_element_type=jnp.float32
    )


def step_order(n, chunks):
    order = [(p, c) for p in range(2, n) for c in range(chunks)]
    head, ahead = order[: chunks * (n - 3) + 3], order[chunks * (n - 3) + 3 :]
    tail = [(n, 0), ahead[0], (n, 1)] + ahead[1:] + [(n, 2)]
    tail += [(n + 1, 0)]
    for c in range(3, chunks):
        tail += [(n, c), (n + 1, c - 2)]
    tail += [(n + 1, c) for c in range(chunks - 2, chunks)]
    return head + tail


def line_kernel(
    n,
    levels,
    q_hbm,
    k_hbm,
    v_hbm,
    res_hbm,
    g_hbm,
    w_hbm,
    mom_hbm,
    doc_hbm,
    step_hbm,
    rb,
    qb,
    kb,
    vb,
    nb,
    mb,
    wbuf,
    gown,
    gpair,
    ctx,
    ctxp,
    cg,
    cgs,
    acc,
    oacc,
    osend,
    ogot,
    rs,
    st,
    pr,
    bias,
    own,
    doc_ref,
    step_ref,
    ds,
    hs,
    ws,
    gs,
    ms,
    ys,
    xg_s,
    xg_r,
    xc_s,
    xc_r,
    xb_s,
    xb_r,
    xo_s,
    xo_r,
    zs,
    zr,
    fs,
    fr,
    ps,
    pr_r,
):
    units, chunks, rows, wide = wbuf.shape
    size = HEAD_SIZE
    tokens, heads = qb.shape[0], qb.shape[1] // size
    per = heads // n
    scale = HEAD_SIZE ** (-0.5)
    me = lax.axis_index("fsdp")
    rep = lax.axis_index("rep")
    z = lax.div(me, 2)
    x = lax.rem(me, 2)
    pair = me + 1 - 2 * x
    at_end = (z == 0) | (z == n - 1)

    def partner(level):
        bit = lax.rem(lax.div(rep, 1 << level), 2)
        return rep + (1 << level) - (2 << level) * bit

    def lanes(c, width):
        return pl.ds(pl.multiple_of(c * width, width), width)

    def own_rows(u):
        return pl.ds(pl.multiple_of((2 * u + x) * rows, 16), rows)

    def pair_rows(u):
        return pl.ds(pl.multiple_of((2 * u + 1 - x) * rows, 16), rows)

    def each_part(c, body):
        @pl.when(c < chunks - 1)
        def _():
            each(COARSE, lambda s: body(c, s, rows // COARSE))

        @pl.when(c == chunks - 1)
        def _():
            each(FINE, lambda s: body(c, s, rows // FINE))

    def cut_rows(s, part):
        return pl.ds(pl.multiple_of(s * part, 16), part)

    def head_rows(h):
        return pl.ds(pl.multiple_of(h * size, size), size)

    def load_head(i, h):
        src = (q_hbm, k_hbm, v_hbm)[i]
        dst = (qb, kb, vb)[i]
        return pltpu.make_async_copy(src.at[:, lanes(h, size)], dst.at[:, lanes(h, size)], hs.at[i, h])

    def load_w(c):
        return pltpu.make_async_copy(w_hbm.at[:, lanes(c, wide)], wbuf.at[z, c], ws.at[c])

    def load_g(c):
        return pltpu.make_async_copy(g_hbm.at[:, lanes(c, wide)], gown.at[c], gs.at[c])

    def load_m(c):
        return pltpu.make_async_copy(mom_hbm.at[:, lanes(c, wide)], mb.at[:, lanes(c, wide)], ms.at[c])

    def load_y(c):
        return pltpu.make_async_copy(res_hbm.at[:, lanes(c, wide)], rb.at[:, lanes(c, wide)], ys.at[c])

    def to_pair(src, dst, send, recv):
        return pltpu.make_async_remote_copy(
            src_ref=src,
            dst_ref=dst,
            send_sem=send,
            recv_sem=recv,
            device_id={"fsdp": pair},
            device_id_type=MESH,
        )

    def x_grad(c):
        return to_pair(g_hbm.at[:, lanes(c, wide)], gpair.at[c], xg_s.at[c], xg_r.at[c])

    def x_context(u):
        return to_pair(ctx.at[pair_rows(u), :], ctxp.at[u], xc_s.at[u], xc_r.at[u])

    def x_back(u):
        return to_pair(cgs.at[u], cg.at[own_rows(u), :], xb_s.at[u], xb_r.at[u])

    def x_out(c):
        return to_pair(osend.at[c], ogot.at[c], xo_s.at[c], xo_r.at[c])

    def along(d, p, c, src, dst):
        return pltpu.make_async_remote_copy(
            src_ref=src,
            dst_ref=dst,
            send_sem=zs.at[d, p - 1, c],
            recv_sem=zr.at[d, p - 1, c],
            device_id={"fsdp": me + 2 - 4 * d},
            device_id_type=MESH,
        )

    def along_last(d, c, s, part, src, dst):
        return pltpu.make_async_remote_copy(
            src_ref=src.at[cut_rows(s, part), :],
            dst_ref=dst.at[cut_rows(s, part), :],
            send_sem=fs.at[d, c, s],
            recv_sem=fr.at[d, c, s],
            device_id={"fsdp": me + 2 - 4 * d},
            device_id_type=MESH,
        )

    def place(d):
        return z + d * (n - 1 - 2 * z)

    def swap(level, c, s, part):
        return pltpu.make_async_remote_copy(
            src_ref=st.at[c, cut_rows(s, part), :],
            dst_ref=pr.at[level, c, cut_rows(s, part), :],
            send_sem=ps.at[level, c, s],
            recv_sem=pr_r.at[level, c, s],
            device_id={"rep": partner(level)},
            device_id_type=MESH,
        )

    def block_at(i):
        return jnp.where(2 * z < n, n - 1 - i, i)

    def each(count, body):
        def run(i, carry):
            body(i)
            return carry

        lax.fori_loop(0, count, run, 0)

    def start_loads(i):
        u = block_at(i)

        def one(hh):
            for a in range(3):
                load_head(a, u * per + hh).start()

        each(per, one)

    barrier = pltpu.get_barrier_semaphore()
    pl.semaphore_signal(barrier, inc=1, device_id={"fsdp": pair}, device_id_type=MESH)
    for level in range(levels):
        pl.semaphore_signal(
            barrier, inc=1, device_id={"rep": partner(level)}, device_id_type=MESH
        )

    @pl.when(z > 0)
    def _():
        pl.semaphore_signal(barrier, inc=1, device_id={"fsdp": me - 2}, device_id_type=MESH)

    @pl.when(z < n - 1)
    def _():
        pl.semaphore_signal(barrier, inc=1, device_id={"fsdp": me + 2}, device_id_type=MESH)

    pl.semaphore_wait(barrier, 1 + levels + jnp.where(at_end, 1, 2))

    def first_sends(c):
        def one(d):
            @pl.when(place(d) < n - 1)
            def _():
                along(d, 1, c, w_hbm.at[:, lanes(c, wide)], wbuf.at[z, c]).start()

        each(2, one)

    each(chunks, first_sends)
    x_grad(0).start()
    load_doc = pltpu.make_async_copy(doc_hbm, doc_ref, ds.at[0])
    load_step = pltpu.make_async_copy(step_hbm, step_ref, ds.at[1])
    load_doc.start()
    load_step.start()
    each(n, start_loads)

    def other_loads(c):
        load_g(c).start()
        load_w(c).start()
        load_m(c).start()
        load_y(c).start()

    each(chunks, other_loads)

    load_doc.wait()
    load_step.wait()
    row_ids = jnp.broadcast_to(doc_ref[...], (tokens, tokens))
    column_ids = jnp.transpose(row_ids)
    r = lax.broadcasted_iota(jnp.int32, (tokens, tokens), 0)
    s = lax.broadcasted_iota(jnp.int32, (tokens, tokens), 1)
    bias[...] = jnp.where((s <= r) & (row_ids == column_ids), 0.0, -jnp.inf)

    blocks = tokens // LANES

    def probabilities_of(q, k, i):
        seen = (i + 1) * LANES
        scores = dot(q[i * LANES : seen], k[:seen], 1, 1) * scale
        scores = scores + bias[i * LANES : seen, :seen]
        exponents = jnp.exp(scores - jnp.max(scores, axis=-1, keepdims=True))
        return exponents * (1.0 / jnp.sum(exponents, axis=-1, keepdims=True))

    def forward_head(h):
        cut_h = lanes(h, size)
        q, k, v = qb[:, cut_h], kb[:, cut_h], vb[:, cut_h]
        parts = []
        for i in range(blocks):
            probs = probabilities_of(q, k, i).astype(jnp.bfloat16)
            parts.append(dot(probs, v[: (i + 1) * LANES], 1, 0))
        context = jnp.concatenate(parts, axis=0)
        ctx[head_rows(h), :] = jnp.transpose(context).astype(jnp.bfloat16)

    def forward_block(i):
        u = block_at(i)

        def one(hh):
            h = u * per + hh
            for a in range(3):
                load_head(a, h).wait()
            forward_head(h)

        each(per, one)
        x_context(u).start()

        @pl.when(i == 0)
        def _():
            each(chunks - 1, lambda c: x_grad(c + 1).start())

    each(n, forward_block)

    def wait_loads(c):
        load_g(c).wait()
        load_w(c).wait()
        load_m(c).wait()
        load_y(c).wait()

    each(chunks, wait_loads)

    def backward_head(h):
        cut_h = lanes(h, size)
        q, k, v = qb[:, cut_h], kb[:, cut_h], vb[:, cut_h]
        grad = jnp.transpose(cg[head_rows(h), :].astype(jnp.float32)).astype(jnp.bfloat16)
        low, score_grads, parts = [], [], []
        for i in range(blocks):
            seen = (i + 1) * LANES
            probs = probabilities_of(q, k, i)
            low.append(probs.astype(jnp.bfloat16))
            prob_grad = dot(grad[i * LANES : seen], v[:seen], 1, 1)
            row_delta = jnp.sum(prob_grad * probs, axis=-1, keepdims=True)
            score_grad = (probs * (prob_grad - row_delta) * scale).astype(jnp.bfloat16)
            score_grads.append(score_grad)
            parts.append(dot(score_grad, k[:seen], 1, 0))
        for i in range(blocks):
            cut = slice(i * LANES, (i + 1) * LANES)
            qb[cut, cut_h] = parts[i].astype(jnp.bfloat16)
        for j in range(blocks):
            cut = slice(j * LANES, (j + 1) * LANES)
            scores_j = jnp.concatenate([b[:, cut] for b in score_grads[j:]], axis=0)
            probs_j = jnp.concatenate([b[:, cut] for b in low[j:]], axis=0)
            kb[cut, cut_h] = dot(scores_j, q[j * LANES :], 0, 0).astype(jnp.bfloat16)
            vb[cut, cut_h] = dot(probs_j, grad[j * LANES :], 0, 0).astype(jnp.bfloat16)

    def backward_heads(u, low, high):
        @pl.when(low == 0)
        def _():
            x_back(u).wait_recv()

        def one(hh, carry):
            backward_head(u * per + hh)
            return carry

        lax.fori_loop(low, high, one, 0)

    def weight_part(u, c):
        return dot(ctx[own_rows(u), :], gown[c], 1, 0) + dot(ctxp[u], gpair[c], 1, 0)

    def unit_chunk(i, u, c):
        weight = wbuf[u, c]
        for side in range(2):
            left = ctx[own_rows(u), :] if side == 0 else ctxp[u]
            grad = gown[c] if side == 0 else gpair[c]
            before = jnp.where(u == z, 0.0, oacc[side, c])
            oacc[side, c] = before + dot(left, weight, 0, 0)
            before = jnp.where(c == 0, 0.0, acc[i, side])
            acc[i, side] = before + dot(weight, grad, 1, 1)

        @pl.when(c == chunks - 1)
        def _():
            cgs[u] = acc[i, 1].astype(jnp.bfloat16)
            cg[own_rows(u), :] = acc[i, 0].astype(jnp.bfloat16)
            x_back(u).start()

    far = jnp.where(2 * z < n, z + 2, z - 2)

    def finish_part(c, s, part):
        def arrived(d):
            @pl.when(place(d) > 0)
            def _():
                along_last(d, c, s, part, rs.at[0, 0], rs.at[0, 0]).wait_recv()

        each(2, arrived)
        cut, across = cut_rows(s, part), lanes(c, wide)
        total = own[cut, :]
        total = total + jnp.where(z > 0, rs[z, c, cut, :].astype(jnp.float32), 0.0)
        total = total + jnp.where(z < n - 1, rs[n, c, cut, :].astype(jnp.float32), 0.0)
        moment = momentum_decay * mb[cut, across] + total
        mb[cut, across] = moment
        stepped = wbuf[z, c, cut, :].astype(jnp.float32) - learning_rate * moment
        st[c, cut, :] = stepped.astype(jnp.bfloat16)
        for level in range(levels):
            swap(level, c, s, part).start()
        a, b = min(2, per), min(3, per)
        u, low, high = pick(
            [
                (at_end & (c == 0) & (s == 1), (far, 0, per)),
                (at_end & (c == chunks - 3) & (s == 1), (last, 0, a)),
                (at_end & (c == chunks - 2) & (s == 0), (last, a, b)),
                (at_end & (c == chunks - 2) & (s == 1), (last, b, min(4, per))),
                (at_end & (c == chunks - 1) & (s == 0), (last, min(4, per), per)),
                (~at_end & (c == 0) & (s == 1), (z + 1, 0, per)),
                (~at_end & (c == 1) & (s == 1), (far, 0, per)),
            ]
        )

        @pl.when(u >= 0)
        def _():
            backward_heads(u, low, high)

    def average(c, s, part):
        cut = cut_rows(s, part)
        for level in range(levels):
            swap(level, c, s, part).wait()
        level_now = jnp.full((part, wide), lax.rem(step_ref[0], levels), jnp.int32)
        other = pr[levels - 1, c, cut, :].astype(jnp.float32)
        for level in range(levels - 1):
            before = pr[level, c, cut, :].astype(jnp.float32)
            other = jnp.where(level_now == level, before, other)
        mean = (st[c, cut, :].astype(jnp.float32) + other) * 0.5
        nb[cut, lanes(c, wide)] = mean.astype(jnp.bfloat16)

    def pick(cases):
        values = (-1, 0, 0)
        for condition, choice in cases:
            values = tuple(jnp.where(condition, a, b) for a, b in zip(choice, values))
        return values

    last = n - 1 - z
    first_side = jnp.where(z > 0, z - 1, z + 1)

    def early_sent(c):
        def line(d):
            @pl.when(place(d) < n - 1)
            def _():
                for p in range(1, n):
                    along(d, p, c, rs.at[0, 0], rs.at[0, 0]).wait_send()

        each(2, line)
        x_grad(c).wait_send()

    def unit_sent(u):
        x_context(u).wait_send()
        x_back(u).wait_send()

    def last_sent(c):
        def line(d):
            @pl.when(place(d) < n - 1)
            def _():
                each_part(
                    c,
                    lambda c, s, part: along_last(
                        d, c, s, part, rs.at[0, 0], rs.at[0, 0]
                    ).wait_send(),
                )

        each(2, line)
        x_out(c).wait_send()

    def finish(c):
        own[...] = weight_part(z, c)
        each_part(c, finish_part)
        x_out(c).wait_recv()
        across = lanes(c, wide)
        total_out = rb[:, across].astype(jnp.float32) + oacc[0, c]
        rb[:, across] = (total_out + ogot[c].astype(jnp.float32)).astype(jnp.bfloat16)

        @pl.when(c > 0)
        def _():
            each_part(c - 1, average)
            last_sent(c - 1)

        @pl.when(c == chunks - 2)
        def _():
            each(chunks, early_sent)

    order = step_order(n, chunks)

    def step(t):
        code = 0
        for i, (p, c) in enumerate(order):
            code = jnp.where(t == i, p * chunks + c, code)
        p = lax.div(code, chunks)
        c = lax.rem(code, chunks)

        @pl.when(p <= n)
        def _():
            def arrived(d):
                @pl.when(place(d) > 0)
                def _():
                    along(d, p - 1, c, rs.at[0, 0], rs.at[0, 0]).wait_recv()

            each(2, arrived)

            def forward(d):
                zz = place(d)

                @pl.when((zz < n - 1) & (p <= zz + 1))
                def _():
                    u = zz + 1 - p
                    u = u + d * (n - 1 - 2 * u)
                    along(d, p, c, wbuf.at[u, c], wbuf.at[u, c]).start()

            each(2, forward)

            @pl.when(p == 2)
            def _():
                x_grad(c).wait_recv()

                @pl.when(c == 0)
                def _():
                    x_context(block_at(0)).wait_recv()

            @pl.when((p == 3) & (c == 0))
            def _():
                each(n - 1, lambda i: x_context(block_at(i + 1)).wait_recv())

            def reduce(d):
                zz = place(d)

                @pl.when((zz < n - 1) & (p > zz + 1))
                def _():
                    b = zz + 1 + n - p
                    b = b + d * (n - 1 - 2 * b)
                    before = jnp.where(zz > 0, rs[b, c].astype(jnp.float32), 0.0)
                    rs[b, c] = (before + weight_part(b, c)).astype(jnp.bfloat16)

                    @pl.when(p < n)
                    def _():
                        along(d, p, c, rs.at[b, c], rs.at[b, c]).start()

                    @pl.when(p == n)
                    def _():
                        slot = jnp.where(d == 1, n, b)
                        each_part(
                            c,
                            lambda c, s, part: along_last(
                                d, c, s, part, rs.at[b, c], rs.at[slot, c]
                            ).start(),
                        )

            each(2, reduce)

        @pl.when((p == 3) | (p == 4))
        def _():
            def unit(i):
                u, low, high = pick(
                    [
                        ((i == 0) & (p == 3) & (c == 0), (z, 0, chunks)),
                        ((i == 0) & (p == 3) & (c == 1), (z - 1, 0, chunks)),
                        ((i == 0) & (p == 3) & (c == 2) & (z < n - 1), (z + 1, 0, chunks)),
                        ((i == 1) & (p == 3), (far, c, c + 1)),
                        ((i == 1) & (p == 4) & at_end, (last, c, c + 1)),
                    ]
                )
                slot = jnp.where(i == 0, 0, p - 2)

                @pl.when(u >= 0)
                def _():
                    def one(cc, carry):
                        unit_chunk(slot, u, cc)
                        return carry

                    lax.fori_loop(low, high, one, 0)

            each(2, unit)

        @pl.when(p == n)
        def _():
            osend[c] = oacc[1, c].astype(jnp.bfloat16)
            x_out(c).start()

            @pl.when((c == 1) | (c == 2))
            def _():
                backward_heads(jnp.where(c == 1, z, first_side), 0, per)

        @pl.when(p == n + 1)
        def _():
            finish(c)

    each(len(order), step)
    each(n, unit_sent)
    each_part(chunks - 1, average)

    last_sent(chunks - 1)


def write_kernel(*refs):
    count = len(refs) // 2
    sems = refs[-1]
    copies = [
        pltpu.make_async_copy(refs[i], refs[count + i], sems.at[i]) for i in range(count)
    ]
    for copy in copies:
        copy.start()
    for copy in copies:
        copy.wait()


def line_shape(count, levels, tokens, features, rows, columns):
    n = count // 2
    heads = features // HEAD_SIZE
    wide = 4 * LANES
    fits = (
        count % 2 == 0
        and n == 4
        and levels >= 1
        and tokens % LANES == 0
        and rows % 16 == 0
        and heads % n == 0
        and 2 * rows * n == features
        and columns % wide == 0
        and columns // wide >= 5
        and rows % (16 * COARSE) == 0
        and rows % (16 * FINE) == 0
    )
    return (n, wide) if fits else None


def on_line(
    n, wide, query, key, value, residual, out_grad, doc_ids, weight, momentum, step_index
):
    tokens, features = query.shape
    rows, columns = weight.shape
    chunks = columns // wide
    heads = features // HEAD_SIZE
    levels = lax.axis_size("rep").bit_length() - 1
    any_space = pl.BlockSpec(memory_space=pl.ANY)
    in_vmem = pl.BlockSpec(memory_space=pltpu.VMEM)
    low, full = jnp.bfloat16, jnp.float32
    dma = pltpu.SemaphoreType.DMA
    like = lambda a: jax.ShapeDtypeStruct(a.shape, a.dtype)
    held = pl.pallas_call(
        functools.partial(line_kernel, n, levels),
        in_specs=[any_space] * 9,
        out_specs=[in_vmem] * 6,
        out_shape=[
            pltpu.VMEM(a.shape, a.dtype)
            for a in (residual, query, key, value, weight, momentum)
        ],
        scratch_shapes=[
            pltpu.VMEM((n, chunks, rows, wide), low),
            pltpu.VMEM((chunks, tokens, wide), low),
            pltpu.VMEM((chunks, tokens, wide), low),
            pltpu.VMEM((features, tokens), low),
            pltpu.VMEM((n, rows, tokens), low),
            pltpu.VMEM((features, tokens), low),
            pltpu.VMEM((n, rows, tokens), low),
            pltpu.VMEM((3, 2, rows, tokens), full),
            pltpu.VMEM((2, chunks, tokens, wide), full),
            pltpu.VMEM((chunks, tokens, wide), low),
            pltpu.VMEM((chunks, tokens, wide), low),
            pltpu.VMEM((n + 1, chunks, rows, wide), low),
            pltpu.VMEM((chunks, rows, wide), low),
            pltpu.VMEM((levels, chunks, rows, wide), low),
            pltpu.VMEM((tokens, tokens), full),
            pltpu.VMEM((rows, wide), full),
            pltpu.VMEM((1, tokens), jnp.int32),
            pltpu.SMEM((1,), jnp.int32),
            dma((2,)),
            dma((3, heads)),
            dma((chunks,)),
            dma((chunks,)),
            dma((chunks,)),
            dma((chunks,)),
            dma((chunks,)),
            dma((chunks,)),
            dma((n,)),
            dma((n,)),
            dma((n,)),
            dma((n,)),
            dma((chunks,)),
            dma((chunks,)),
            dma((2, n - 1, chunks)),
            dma((2, n - 1, chunks)),
            dma((2, chunks, FINE)),
            dma((2, chunks, FINE)),
            dma((levels, chunks, FINE)),
            dma((levels, chunks, FINE)),
        ],
        compiler_params=pltpu.CompilerParams(
            collective_id=0, has_side_effects=True, vmem_limit_bytes=50 << 20
        ),
    )(
        query,
        key,
        value,
        residual,
        out_grad,
        weight,
        momentum,
        doc_ids,
        step_index,
    )
    return pl.pallas_call(
        write_kernel,
        in_specs=[any_space] * 6,
        out_specs=[any_space] * 6,
        out_shape=[like(a) for a in (residual, query, key, value, weight, momentum)],
        scratch_shapes=[dma((6,))],
        compiler_params=pltpu.CompilerParams(vmem_limit_bytes=1 << 20),
    )(*held)


def on_device(
    query_rows,
    key_rows,
    value_rows,
    residual_in,
    out_grad,
    doc_ids,
    out_weight,
    momentum,
    step_index,
):
    count = lax.axis_size("fsdp")
    shape = line_shape(
        count,
        lax.axis_size("rep").bit_length() - 1,
        query_rows.shape[1],
        query_rows.shape[2],
        out_weight.shape[1],
        out_weight.shape[2],
    )
    if shape is not None:
        arrays = (query_rows, key_rows, value_rows, residual_in, out_grad)
        results = on_line(
            *shape, *[a[0] for a in arrays], doc_ids, out_weight[0], momentum[0], step_index
        )
        return tuple(r[None] for r in results)
    side = lax.axis_index("fsdp") % 2
    groups = [[i for i in range(count) if i % 2 == s] for s in range(2)]
    pair = [(i, i ^ 1) for i in range(count)]
    first = side == 0
    query, key, value = query_rows[0], key_rows[0], value_rows[0]
    weight_shard = out_weight[0]
    own_grad = out_grad[0]
    rows = weight_shard.shape[0]
    gathered = lax.all_gather(
        weight_shard, "fsdp", axis=0, tiled=True, axis_index_groups=groups
    )
    pair_grad = lax.ppermute(own_grad, "fsdp", pair)
    (context,) = per_head(forward_kernel, (query, key, value), doc_ids[0], 1, 2)

    def half(array, which):
        return jnp.concatenate(
            [array[:, j * rows : (j + 1) * rows] for j in range(which, count, 2)], axis=1
        )

    low, high = half(context, 0), half(context, 1)
    own_context = jnp.where(first, low, high)
    pair_context = lax.ppermute(jnp.where(first, high, low), "fsdp", pair)

    def outer(left, right):
        return lax.dot_general(
            left, right, (((0,), (0,)), ((), ())), preferred_element_type=jnp.float32
        )

    weight_term = (outer(own_context, own_grad) + outer(pair_context, pair_grad)).astype(
        jnp.bfloat16
    )
    weight_grad = lax.psum_scatter(
        weight_term, "fsdp", scatter_dimension=0, tiled=True, axis_index_groups=groups
    ).astype(jnp.float32)

    def back(grad):
        return lax.dot_general(
            grad, gathered, (((1,), (1,)), ((), ())), preferred_element_type=jnp.float32
        ).astype(jnp.bfloat16)

    got_back = lax.ppermute(back(pair_grad), "fsdp", pair)
    pair_out = jnp.dot(pair_context, gathered, preferred_element_type=jnp.float32)
    got_out = lax.ppermute(pair_out.astype(jnp.bfloat16), "fsdp", pair)
    own_back = back(own_grad)
    even = jnp.where(first, own_back, got_back)
    odd = jnp.where(first, got_back, own_back)
    pieces = []
    for j in range(count // 2):
        cut = slice(j * rows, (j + 1) * rows)
        pieces += [even[:, cut], odd[:, cut]]
    context_grad = jnp.concatenate(pieces, axis=1)
    query_grad, key_grad, value_grad = per_head(
        backward_kernel, (query, key, value, context_grad), doc_ids[0], 3, 5
    )
    own_out = jnp.dot(own_context, gathered, preferred_element_type=jnp.float32)
    block_out = (
        residual_in[0].astype(jnp.float32) + own_out + got_out.astype(jnp.float32)
    ).astype(jnp.bfloat16)

    new_momentum = momentum_decay * momentum[0] + weight_grad
    stepped = (weight_shard.astype(jnp.float32) - learning_rate * new_momentum).astype(jnp.bfloat16)
    levels = lax.axis_size("rep").bit_length() - 1
    branches = [functools.partial(swapped, axis="rep", distance=level) for level in range(levels)]
    partner = lax.switch(step_index[0] % levels, branches, stepped)
    new_weight = ((stepped.astype(jnp.float32) + partner.astype(jnp.float32)) * 0.5).astype(
        jnp.bfloat16
    )
    return (
        block_out[None],
        query_grad[None],
        key_grad[None],
        value_grad[None],
        new_weight[None],
        new_momentum[None],
    )


def solution(mesh):
    rows = P("rep", "fsdp", None)
    return jax.shard_map(
        on_device,
        mesh=mesh,
        in_specs=(rows, rows, rows, rows, rows, P("rep", "fsdp"), rows, rows, P()),
        out_specs=(rows,) * 6,
        check_vma=False,
    )
```

```python
import functools

import jax
import jax.numpy as jnp
from jax import lax
from jax.experimental import pallas as pl
from jax.experimental.pallas import tpu as pltpu
from jax.sharding import PartitionSpec as P

HEAD_SIZE = 128

momentum_decay = 0.9
learning_rate = 0.0003


def swapped(block, axis, distance):
    count = lax.axis_size(axis)
    route = []
    for low in range(count):
        high = low | 1 << distance
        if high != low and high < count:
            route += [(low, high), (high, low)]
    return lax.ppermute(block, axis, route)


def probabilities(q, k, doc_column, doc_row):
    length = q.shape[0]
    scores = lax.dot_general(
        q, k, (((1,), (1,)), ((), ())), preferred_element_type=jnp.float32
    ) * (HEAD_SIZE ** (-0.5))
    rows = lax.broadcasted_iota(jnp.int32, (length, length), 0)
    columns = lax.broadcasted_iota(jnp.int32, (length, length), 1)
    allowed = (columns <= rows) & (doc_column == doc_row)
    scores = jnp.where(allowed, scores, -jnp.inf)
    exponents = jnp.exp(scores - jnp.max(scores, axis=-1, keepdims=True))
    return exponents / jnp.sum(exponents, axis=-1, keepdims=True)


def forward_kernel(q_ref, k_ref, v_ref, doc_column_ref, doc_row_ref, context_ref):
    for head in range(q_ref.shape[1] // HEAD_SIZE):
        cut = slice(head * HEAD_SIZE, (head + 1) * HEAD_SIZE)
        probs = probabilities(q_ref[:, cut], k_ref[:, cut], doc_column_ref[...], doc_row_ref[...])
        context_ref[:, cut] = jnp.dot(
            probs.astype(jnp.bfloat16), v_ref[:, cut], preferred_element_type=jnp.float32
        ).astype(jnp.bfloat16)


def backward_kernel(
    q_ref, k_ref, v_ref, grad_ref, doc_column_ref, doc_row_ref, dq_ref, dk_ref, dv_ref
):
    for head in range(q_ref.shape[1] // HEAD_SIZE):
        cut = slice(head * HEAD_SIZE, (head + 1) * HEAD_SIZE)
        q, k, v, grad = q_ref[:, cut], k_ref[:, cut], v_ref[:, cut], grad_ref[:, cut]
        probs = probabilities(q, k, doc_column_ref[...], doc_row_ref[...])
        dv_ref[:, cut] = lax.dot_general(
            probs.astype(jnp.bfloat16),
            grad,
            (((0,), (0,)), ((), ())),
            preferred_element_type=jnp.float32,
        ).astype(jnp.bfloat16)
        prob_grad = lax.dot_general(
            grad, v, (((1,), (1,)), ((), ())), preferred_element_type=jnp.float32
        )
        row_delta = jnp.sum(prob_grad * probs, axis=-1, keepdims=True)
        score_grad = (probs * (prob_grad - row_delta) * (HEAD_SIZE ** (-0.5))).astype(jnp.bfloat16)
        dq_ref[:, cut] = jnp.dot(score_grad, k, preferred_element_type=jnp.float32).astype(
            jnp.bfloat16
        )
        dk_ref[:, cut] = lax.dot_general(
            score_grad, q, (((0,), (0,)), ((), ())), preferred_element_type=jnp.float32
        ).astype(jnp.bfloat16)


def per_head(kernel, arrays, doc_block, outputs, matmuls):
    length, width = arrays[0].shape
    step = 2 * HEAD_SIZE if width % (2 * HEAD_SIZE) == 0 else HEAD_SIZE
    block = pl.BlockSpec((length, step), lambda h: (0, h))
    whole = lambda shape: pl.BlockSpec(shape, lambda h: (0, 0))
    result = jax.ShapeDtypeStruct((length, width), jnp.bfloat16)
    return pl.pallas_call(
        kernel,
        grid=(width // step,),
        in_specs=[block] * len(arrays) + [whole((length, 1)), whole((1, length))],
        out_specs=[block] * outputs,
        out_shape=[result] * outputs,
        cost_estimate=pl.CostEstimate(
            flops=4 * matmuls * length * length * width,
            bytes_accessed=(len(arrays) + outputs) * length * width * 2,
            transcendentals=length * length * width // HEAD_SIZE,
        ),
    )(*arrays, doc_block[:, None], doc_block[None, :])


MESH = pl.DeviceIdType.MESH
LANES = 128
PARTS = ((1, 2), (2, 2))


def dot(a, b, ca, cb):
    return lax.dot_general(
        a, b, (((ca,), (cb,)), ((), ())), preferred_element_type=jnp.float32
    )


def step_order(n, chunks):
    order = [(p, c) for p in range(2, n) for c in range(chunks)]
    head, ahead = order[: chunks * (n - 3) + 3], order[chunks * (n - 3) + 3 :]
    tail = [(n, 0), ahead[0], (n, 1)] + ahead[1:] + [(n, 2)]
    tail += [(n + 1, 0)]
    for c in range(3, chunks):
        tail += [(n, c), (n + 1, c - 2)]
    tail += [(n + 1, c) for c in range(chunks - 2, chunks)]
    return head + tail


def line_kernel(
    n,
    level,
    q_hbm,
    k_hbm,
    v_hbm,
    res_hbm,
    g_hbm,
    w_hbm,
    mom_hbm,
    doc_hbm,
    rb,
    qb,
    kb,
    vb,
    nb,
    mb,
    wbuf,
    gown,
    gpair,
    ctx,
    ctxp,
    cg,
    cgs,
    acc,
    oacc,
    osend,
    ogot,
    rs,
    st,
    pr,
    bias,
    own,
    doc_ref,
    ds,
    hs,
    ws,
    gs,
    ms,
    ys,
    xg_s,
    xg_r,
    xc_s,
    xc_r,
    xb_s,
    xb_r,
    xo_s,
    xo_r,
    zs,
    zr,
    fs,
    fr,
    ps,
    pr_r,
):
    units, chunks, rows, wide = wbuf.shape
    size = HEAD_SIZE
    tokens, heads = qb.shape[0], qb.shape[1] // size
    per = heads // n
    coarse, fine = PARTS[min(level, 1)]
    scale = HEAD_SIZE ** (-0.5)
    me = lax.axis_index("fsdp")
    rep = lax.axis_index("rep")
    z = lax.div(me, 2)
    x = lax.rem(me, 2)
    pair = me + 1 - 2 * x
    at_end = (z == 0) | (z == n - 1)

    bit = lax.rem(lax.div(rep, 1 << level), 2)
    partner = rep + (1 << level) - (2 << level) * bit

    def lanes(c, width):
        return pl.ds(pl.multiple_of(c * width, width), width)

    def own_rows(u):
        return pl.ds(pl.multiple_of((2 * u + x) * rows, 16), rows)

    def pair_rows(u):
        return pl.ds(pl.multiple_of((2 * u + 1 - x) * rows, 16), rows)

    def each_part(c, body):
        @pl.when(c < chunks - 1)
        def _():
            each(coarse, lambda s: body(c, s, rows // coarse))

        @pl.when(c == chunks - 1)
        def _():
            each(fine, lambda s: body(c, s, rows // fine))

    def cut_rows(s, part):
        return pl.ds(pl.multiple_of(s * part, 16), part)

    def head_rows(h):
        return pl.ds(pl.multiple_of(h * size, size), size)

    def load_head(i, h):
        src = (q_hbm, k_hbm, v_hbm)[i]
        dst = (qb, kb, vb)[i]
        return pltpu.make_async_copy(src.at[:, lanes(h, size)], dst.at[:, lanes(h, size)], hs.at[i, h])

    def load_w(c):
        return pltpu.make_async_copy(w_hbm.at[:, lanes(c, wide)], wbuf.at[z, c], ws.at[c])

    def load_g(c):
        return pltpu.make_async_copy(g_hbm.at[:, lanes(c, wide)], gown.at[c], gs.at[c])

    def load_m(c):
        return pltpu.make_async_copy(mom_hbm.at[:, lanes(c, wide)], mb.at[:, lanes(c, wide)], ms.at[c])

    def load_y(c):
        return pltpu.make_async_copy(res_hbm.at[:, lanes(c, wide)], rb.at[:, lanes(c, wide)], ys.at[c])

    def to_pair(src, dst, send, recv):
        return pltpu.make_async_remote_copy(
            src_ref=src,
            dst_ref=dst,
            send_sem=send,
            recv_sem=recv,
            device_id={"fsdp": pair},
            device_id_type=MESH,
        )

    def x_grad(c):
        return to_pair(g_hbm.at[:, lanes(c, wide)], gpair.at[c], xg_s.at[c], xg_r.at[c])

    def x_context(u):
        return to_pair(ctx.at[pair_rows(u), :], ctxp.at[u], xc_s.at[u], xc_r.at[u])

    def x_back(u):
        return to_pair(cgs.at[u], cg.at[own_rows(u), :], xb_s.at[u], xb_r.at[u])

    def x_out(c):
        return to_pair(osend.at[c], ogot.at[c], xo_s.at[c], xo_r.at[c])

    def along(d, p, c, src, dst):
        return pltpu.make_async_remote_copy(
            src_ref=src,
            dst_ref=dst,
            send_sem=zs.at[d, p - 1, c],
            recv_sem=zr.at[d, p - 1, c],
            device_id={"fsdp": me + 2 - 4 * d},
            device_id_type=MESH,
        )

    def along_last(d, c, s, part, src, dst):
        return pltpu.make_async_remote_copy(
            src_ref=src.at[cut_rows(s, part), :],
            dst_ref=dst.at[cut_rows(s, part), :],
            send_sem=fs.at[d, c, s],
            recv_sem=fr.at[d, c, s],
            device_id={"fsdp": me + 2 - 4 * d},
            device_id_type=MESH,
        )

    def place(d):
        return z + d * (n - 1 - 2 * z)

    def swap(c, s, part):
        return pltpu.make_async_remote_copy(
            src_ref=st.at[c, cut_rows(s, part), :],
            dst_ref=pr.at[c, cut_rows(s, part), :],
            send_sem=ps.at[c, s],
            recv_sem=pr_r.at[c, s],
            device_id={"rep": partner},
            device_id_type=MESH,
        )

    def block_at(i):
        return jnp.where(2 * z < n, n - 1 - i, i)

    def each(count, body):
        def run(i, carry):
            body(i)
            return carry

        lax.fori_loop(0, count, run, 0)

    def start_loads(i):
        u = block_at(i)

        def one(hh):
            for a in range(3):
                load_head(a, u * per + hh).start()

        each(per, one)

    barrier = pltpu.get_barrier_semaphore()
    pl.semaphore_signal(barrier, inc=1, device_id={"fsdp": pair}, device_id_type=MESH)
    pl.semaphore_signal(barrier, inc=1, device_id={"rep": partner}, device_id_type=MESH)

    @pl.when(z > 0)
    def _():
        pl.semaphore_signal(barrier, inc=1, device_id={"fsdp": me - 2}, device_id_type=MESH)

    @pl.when(z < n - 1)
    def _():
        pl.semaphore_signal(barrier, inc=1, device_id={"fsdp": me + 2}, device_id_type=MESH)

    pl.semaphore_wait(barrier, 2 + jnp.where(at_end, 1, 2))

    def first_sends(c):
        def one(d):
            @pl.when(place(d) < n - 1)
            def _():
                along(d, 1, c, w_hbm.at[:, lanes(c, wide)], wbuf.at[z, c]).start()

        each(2, one)

    each(chunks, first_sends)
    x_grad(0).start()
    load_doc = pltpu.make_async_copy(doc_hbm, doc_ref, ds)
    load_doc.start()
    each(n, start_loads)

    def other_loads(c):
        load_g(c).start()
        load_w(c).start()
        load_m(c).start()
        load_y(c).start()

    each(chunks, other_loads)

    load_doc.wait()
    row_ids = jnp.broadcast_to(doc_ref[...], (tokens, tokens))
    column_ids = jnp.transpose(row_ids)
    r = lax.broadcasted_iota(jnp.int32, (tokens, tokens), 0)
    s = lax.broadcasted_iota(jnp.int32, (tokens, tokens), 1)
    bias[...] = jnp.where((s <= r) & (row_ids == column_ids), 0.0, -jnp.inf)

    blocks = tokens // LANES

    def probabilities_of(q, k, i):
        seen = (i + 1) * LANES
        scores = dot(q[i * LANES : seen], k[:seen], 1, 1) * scale
        scores = scores + bias[i * LANES : seen, :seen]
        exponents = jnp.exp(scores - jnp.max(scores, axis=-1, keepdims=True))
        return exponents * (1.0 / jnp.sum(exponents, axis=-1, keepdims=True))

    def forward_head(h):
        cut_h = lanes(h, size)
        q, k, v = qb[:, cut_h], kb[:, cut_h], vb[:, cut_h]
        parts = []
        for i in range(blocks):
            probs = probabilities_of(q, k, i).astype(jnp.bfloat16)
            parts.append(dot(probs, v[: (i + 1) * LANES], 1, 0))
        context = jnp.concatenate(parts, axis=0)
        ctx[head_rows(h), :] = jnp.transpose(context).astype(jnp.bfloat16)

    def forward_block(i):
        u = block_at(i)

        def one(hh):
            h = u * per + hh
            for a in range(3):
                load_head(a, h).wait()
            forward_head(h)

        each(per, one)
        x_context(u).start()

        @pl.when(i == 0)
        def _():
            each(chunks - 1, lambda c: x_grad(c + 1).start())

    each(n, forward_block)

    def wait_loads(c):
        load_g(c).wait()
        load_w(c).wait()
        load_m(c).wait()
        load_y(c).wait()

    each(chunks, wait_loads)

    def backward_head(h):
        cut_h = lanes(h, size)
        q, k, v = qb[:, cut_h], kb[:, cut_h], vb[:, cut_h]
        grad = jnp.transpose(cg[head_rows(h), :].astype(jnp.float32)).astype(jnp.bfloat16)
        low, score_grads, parts = [], [], []
        for i in range(blocks):
            seen = (i + 1) * LANES
            probs = probabilities_of(q, k, i)
            low.append(probs.astype(jnp.bfloat16))
            prob_grad = dot(grad[i * LANES : seen], v[:seen], 1, 1)
            row_delta = jnp.sum(prob_grad * probs, axis=-1, keepdims=True)
            score_grad = (probs * (prob_grad - row_delta) * scale).astype(jnp.bfloat16)
            score_grads.append(score_grad)
            parts.append(dot(score_grad, k[:seen], 1, 0))
        for i in range(blocks):
            cut = slice(i * LANES, (i + 1) * LANES)
            qb[cut, cut_h] = parts[i].astype(jnp.bfloat16)
        for j in range(blocks):
            cut = slice(j * LANES, (j + 1) * LANES)
            scores_j = jnp.concatenate([b[:, cut] for b in score_grads[j:]], axis=0)
            probs_j = jnp.concatenate([b[:, cut] for b in low[j:]], axis=0)
            kb[cut, cut_h] = dot(scores_j, q[j * LANES :], 0, 0).astype(jnp.bfloat16)
            vb[cut, cut_h] = dot(probs_j, grad[j * LANES :], 0, 0).astype(jnp.bfloat16)

    def backward_heads(u, low, high):
        @pl.when(low == 0)
        def _():
            x_back(u).wait_recv()

        def one(hh, carry):
            backward_head(u * per + hh)
            return carry

        lax.fori_loop(low, high, one, 0)

    def weight_part(u, c):
        return dot(ctx[own_rows(u), :], gown[c], 1, 0) + dot(ctxp[u], gpair[c], 1, 0)

    def unit_chunk(i, u, c):
        weight = wbuf[u, c]
        for side in range(2):
            left = ctx[own_rows(u), :] if side == 0 else ctxp[u]
            grad = gown[c] if side == 0 else gpair[c]
            before = jnp.where(u == z, 0.0, oacc[side, c])
            oacc[side, c] = before + dot(left, weight, 0, 0)
            before = jnp.where(c == 0, 0.0, acc[i, side])
            acc[i, side] = before + dot(weight, grad, 1, 1)

        @pl.when(c == chunks - 1)
        def _():
            cgs[u] = acc[i, 1].astype(jnp.bfloat16)
            cg[own_rows(u), :] = acc[i, 0].astype(jnp.bfloat16)
            x_back(u).start()

    far = jnp.where(2 * z < n, z + 2, z - 2)

    def finish_part(c, s, part):
        def arrived(d):
            @pl.when(place(d) > 0)
            def _():
                along_last(d, c, s, part, rs.at[0, 0], rs.at[0, 0]).wait_recv()

        each(2, arrived)
        cut, across = cut_rows(s, part), lanes(c, wide)
        total = own[cut, :]
        total = total + jnp.where(z > 0, rs[z, c, cut, :].astype(jnp.float32), 0.0)
        total = total + jnp.where(z < n - 1, rs[n, c, cut, :].astype(jnp.float32), 0.0)
        moment = momentum_decay * mb[cut, across] + total
        mb[cut, across] = moment
        stepped = wbuf[z, c, cut, :].astype(jnp.float32) - learning_rate * moment
        st[c, cut, :] = stepped.astype(jnp.bfloat16)
        swap(c, s, part).start()
        a, b, e = min(2, per), min(3, per), min(4, per)
        tip = coarse - 1
        u, low, high = pick(
            [
                (at_end & (c == 0) & (s == tip), (far, 0, per)),
                (at_end & (c == chunks - 3) & (s == tip), (last, 0, a)),
                (at_end & (c == chunks - 2) & (s == 0), (last, a, e if coarse == 1 else b)),
                (at_end & (c == chunks - 2) & (s == 1), (last, b, e)),
                (at_end & (c == chunks - 1) & (s == fine - 1), (last, e, per)),
                (~at_end & (c == 0) & (s == tip), (z + 1, 0, per)),
                (~at_end & (c == 1) & (s == tip), (far, 0, per)),
            ]
        )

        @pl.when(u >= 0)
        def _():
            backward_heads(u, low, high)

    def average(c, s, part):
        cut = cut_rows(s, part)
        swap(c, s, part).wait()
        other = pr[c, cut, :].astype(jnp.float32)
        mean = (st[c, cut, :].astype(jnp.float32) + other) * 0.5
        nb[cut, lanes(c, wide)] = mean.astype(jnp.bfloat16)

    def pick(cases):
        values = (-1, 0, 0)
        for condition, choice in cases:
            values = tuple(jnp.where(condition, a, b) for a, b in zip(choice, values))
        return values

    last = n - 1 - z
    first_side = jnp.where(z > 0, z - 1, z + 1)

    def early_sent(c):
        def line(d):
            @pl.when(place(d) < n - 1)
            def _():
                for p in range(1, n):
                    along(d, p, c, rs.at[0, 0], rs.at[0, 0]).wait_send()

        each(2, line)
        x_grad(c).wait_send()

    def unit_sent(u):
        x_context(u).wait_send()
        x_back(u).wait_send()

    def last_sent(c):
        def line(d):
            @pl.when(place(d) < n - 1)
            def _():
                each_part(
                    c,
                    lambda c, s, part: along_last(
                        d, c, s, part, rs.at[0, 0], rs.at[0, 0]
                    ).wait_send(),
                )

        each(2, line)
        x_out(c).wait_send()

    def finish(c):
        own[...] = weight_part(z, c)
        each_part(c, finish_part)

        @pl.when(c < chunks - 2)
        def _():
            finish_out(c)

        @pl.when((c > 0) & (c < chunks - 2))
        def _():
            each_part(c - 1, average)
            last_sent(c - 1)

        @pl.when(c == chunks - 1)
        def _():
            finish_out(chunks - 2)
            finish_out(chunks - 1)
            for i in (3, 2):
                each_part(chunks - i, average)
                last_sent(chunks - i)
            each(chunks, early_sent)
            each(n, unit_sent)

    def finish_out(c):
        x_out(c).wait_recv()
        across = lanes(c, wide)
        total_out = rb[:, across].astype(jnp.float32) + oacc[0, c]
        rb[:, across] = (total_out + ogot[c].astype(jnp.float32)).astype(jnp.bfloat16)

    order = step_order(n, chunks)

    def step(t):
        code = 0
        for i, (p, c) in enumerate(order):
            code = jnp.where(t == i, p * chunks + c, code)
        p = lax.div(code, chunks)
        c = lax.rem(code, chunks)

        @pl.when(p <= n)
        def _():
            def arrived(d):
                @pl.when(place(d) > 0)
                def _():
                    along(d, p - 1, c, rs.at[0, 0], rs.at[0, 0]).wait_recv()

            each(2, arrived)

            def forward(d):
                zz = place(d)

                @pl.when((zz < n - 1) & (p <= zz + 1))
                def _():
                    u = zz + 1 - p
                    u = u + d * (n - 1 - 2 * u)
                    along(d, p, c, wbuf.at[u, c], wbuf.at[u, c]).start()

            each(2, forward)

            @pl.when(p == 2)
            def _():
                x_grad(c).wait_recv()

                @pl.when(c == 0)
                def _():
                    x_context(block_at(0)).wait_recv()

            @pl.when((p == 3) & (c == 0))
            def _():
                each(n - 1, lambda i: x_context(block_at(i + 1)).wait_recv())

            def reduce(d):
                zz = place(d)

                @pl.when((zz < n - 1) & (p > zz + 1))
                def _():
                    b = zz + 1 + n - p
                    b = b + d * (n - 1 - 2 * b)
                    before = jnp.where(zz > 0, rs[b, c].astype(jnp.float32), 0.0)
                    rs[b, c] = (before + weight_part(b, c)).astype(jnp.bfloat16)

                    @pl.when(p < n)
                    def _():
                        along(d, p, c, rs.at[b, c], rs.at[b, c]).start()

                    @pl.when(p == n)
                    def _():
                        slot = jnp.where(d == 1, n, b)
                        each_part(
                            c,
                            lambda c, s, part: along_last(
                                d, c, s, part, rs.at[b, c], rs.at[slot, c]
                            ).start(),
                        )

            each(2, reduce)

        @pl.when((p == 3) | (p == 4))
        def _():
            def unit(i):
                u, low, high = pick(
                    [
                        ((i == 0) & (p == 3) & (c == 0), (z, 0, chunks)),
                        ((i == 0) & (p == 3) & (c == 1), (z - 1, 0, chunks)),
                        ((i == 0) & (p == 3) & (c == 2) & (z < n - 1), (z + 1, 0, chunks)),
                        ((i == 1) & (p == 3), (far, c, c + 1)),
                        ((i == 1) & (p == 4) & at_end, (last, c, c + 1)),
                    ]
                )
                slot = jnp.where(i == 0, 0, p - 2)

                @pl.when(u >= 0)
                def _():
                    def one(cc, carry):
                        unit_chunk(slot, u, cc)
                        return carry

                    lax.fori_loop(low, high, one, 0)

            each(2, unit)

        @pl.when(p == n)
        def _():
            osend[c] = oacc[1, c].astype(jnp.bfloat16)
            x_out(c).start()

            @pl.when((c == 1) | (c == 2))
            def _():
                backward_heads(jnp.where(c == 1, z, first_side), 0, per)

        @pl.when(p == n + 1)
        def _():
            finish(c)

    each(len(order), step)
    each_part(chunks - 1, average)

    last_sent(chunks - 1)


def write_kernel(*refs):
    count = len(refs) // 2
    sems = refs[-1]
    copies = [
        pltpu.make_async_copy(refs[i], refs[count + i], sems.at[i]) for i in range(count)
    ]
    for copy in copies:
        copy.start()
    for copy in copies:
        copy.wait()


def line_shape(count, levels, tokens, features, rows, columns):
    n = count // 2
    heads = features // HEAD_SIZE
    wide = 4 * LANES
    fits = (
        count % 2 == 0
        and n == 4
        and levels >= 1
        and tokens % LANES == 0
        and rows % 16 == 0
        and heads % n == 0
        and 2 * rows * n == features
        and columns % wide == 0
        and columns // wide >= 5
        and all(rows % (16 * part) == 0 for parts in PARTS for part in parts)
    )
    return (n, wide) if fits else None


def on_line(
    n, wide, level, query, key, value, residual, out_grad, doc_ids, weight, momentum
):
    tokens, features = query.shape
    rows, columns = weight.shape
    chunks = columns // wide
    heads = features // HEAD_SIZE
    any_space = pl.BlockSpec(memory_space=pl.ANY)
    in_vmem = pl.BlockSpec(memory_space=pltpu.VMEM)
    fine = max(PARTS[min(level, 1)])
    low, full = jnp.bfloat16, jnp.float32
    dma = pltpu.SemaphoreType.DMA
    like = lambda a: jax.ShapeDtypeStruct(a.shape, a.dtype)
    held = pl.pallas_call(
        functools.partial(line_kernel, n, level),
        in_specs=[any_space] * 8,
        out_specs=[in_vmem] * 6,
        out_shape=[
            pltpu.VMEM(a.shape, a.dtype)
            for a in (residual, query, key, value, weight, momentum)
        ],
        scratch_shapes=[
            pltpu.VMEM((n, chunks, rows, wide), low),
            pltpu.VMEM((chunks, tokens, wide), low),
            pltpu.VMEM((chunks, tokens, wide), low),
            pltpu.VMEM((features, tokens), low),
            pltpu.VMEM((n, rows, tokens), low),
            pltpu.VMEM((features, tokens), low),
            pltpu.VMEM((n, rows, tokens), low),
            pltpu.VMEM((3, 2, rows, tokens), full),
            pltpu.VMEM((2, chunks, tokens, wide), full),
            pltpu.VMEM((chunks, tokens, wide), low),
            pltpu.VMEM((chunks, tokens, wide), low),
            pltpu.VMEM((n + 1, chunks, rows, wide), low),
            pltpu.VMEM((chunks, rows, wide), low),
            pltpu.VMEM((chunks, rows, wide), low),
            pltpu.VMEM((tokens, tokens), full),
            pltpu.VMEM((rows, wide), full),
            pltpu.VMEM((1, tokens), jnp.int32),
            dma(()),
            dma((3, heads)),
            dma((chunks,)),
            dma((chunks,)),
            dma((chunks,)),
            dma((chunks,)),
            dma((chunks,)),
            dma((chunks,)),
            dma((n,)),
            dma((n,)),
            dma((n,)),
            dma((n,)),
            dma((chunks,)),
            dma((chunks,)),
            dma((2, n - 1, chunks)),
            dma((2, n - 1, chunks)),
            dma((2, chunks, fine)),
            dma((2, chunks, fine)),
            dma((chunks, fine)),
            dma((chunks, fine)),
        ],
        compiler_params=pltpu.CompilerParams(
            collective_id=level, has_side_effects=True, vmem_limit_bytes=50 << 20
        ),
    )(
        query,
        key,
        value,
        residual,
        out_grad,
        weight,
        momentum,
        doc_ids,
    )
    return pl.pallas_call(
        write_kernel,
        in_specs=[any_space] * 6,
        out_specs=[any_space] * 6,
        out_shape=[like(a) for a in (residual, query, key, value, weight, momentum)],
        scratch_shapes=[dma((6,))],
        compiler_params=pltpu.CompilerParams(vmem_limit_bytes=1 << 20),
    )(*held)


def on_device(
    query_rows,
    key_rows,
    value_rows,
    residual_in,
    out_grad,
    doc_ids,
    out_weight,
    momentum,
    step_index,
):
    count = lax.axis_size("fsdp")
    shape = line_shape(
        count,
        lax.axis_size("rep").bit_length() - 1,
        query_rows.shape[1],
        query_rows.shape[2],
        out_weight.shape[1],
        out_weight.shape[2],
    )
    if shape is not None:
        arrays = (query_rows, key_rows, value_rows, residual_in, out_grad)
        levels = lax.axis_size("rep").bit_length() - 1
        results = lax.switch(
            lax.rem(step_index[0].astype(jnp.uint32), jnp.uint32(levels)).astype(jnp.int32),
            [functools.partial(on_line, *shape, level) for level in range(levels)],
            *[a[0] for a in arrays],
            doc_ids,
            out_weight[0],
            momentum[0],
        )
        return tuple(r[None] for r in results)
    side = lax.axis_index("fsdp") % 2
    groups = [[i for i in range(count) if i % 2 == s] for s in range(2)]
    pair = [(i, i ^ 1) for i in range(count)]
    first = side == 0
    query, key, value = query_rows[0], key_rows[0], value_rows[0]
    weight_shard = out_weight[0]
    own_grad = out_grad[0]
    rows = weight_shard.shape[0]
    gathered = lax.all_gather(
        weight_shard, "fsdp", axis=0, tiled=True, axis_index_groups=groups
    )
    pair_grad = lax.ppermute(own_grad, "fsdp", pair)
    (context,) = per_head(forward_kernel, (query, key, value), doc_ids[0], 1, 2)

    def half(array, which):
        return jnp.concatenate(
            [array[:, j * rows : (j + 1) * rows] for j in range(which, count, 2)], axis=1
        )

    low, high = half(context, 0), half(context, 1)
    own_context = jnp.where(first, low, high)
    pair_context = lax.ppermute(jnp.where(first, high, low), "fsdp", pair)

    def outer(left, right):
        return lax.dot_general(
            left, right, (((0,), (0,)), ((), ())), preferred_element_type=jnp.float32
        )

    weight_term = (outer(own_context, own_grad) + outer(pair_context, pair_grad)).astype(
        jnp.bfloat16
    )
    weight_grad = lax.psum_scatter(
        weight_term, "fsdp", scatter_dimension=0, tiled=True, axis_index_groups=groups
    ).astype(jnp.float32)

    def back(grad):
        return lax.dot_general(
            grad, gathered, (((1,), (1,)), ((), ())), preferred_element_type=jnp.float32
        ).astype(jnp.bfloat16)

    got_back = lax.ppermute(back(pair_grad), "fsdp", pair)
    pair_out = jnp.dot(pair_context, gathered, preferred_element_type=jnp.float32)
    got_out = lax.ppermute(pair_out.astype(jnp.bfloat16), "fsdp", pair)
    own_back = back(own_grad)
    even = jnp.where(first, own_back, got_back)
    odd = jnp.where(first, got_back, own_back)
    pieces = []
    for j in range(count // 2):
        cut = slice(j * rows, (j + 1) * rows)
        pieces += [even[:, cut], odd[:, cut]]
    context_grad = jnp.concatenate(pieces, axis=1)
    query_grad, key_grad, value_grad = per_head(
        backward_kernel, (query, key, value, context_grad), doc_ids[0], 3, 5
    )
    own_out = jnp.dot(own_context, gathered, preferred_element_type=jnp.float32)
    block_out = (
        residual_in[0].astype(jnp.float32) + own_out + got_out.astype(jnp.float32)
    ).astype(jnp.bfloat16)

    new_momentum = momentum_decay * momentum[0] + weight_grad
    stepped = (weight_shard.astype(jnp.float32) - learning_rate * new_momentum).astype(jnp.bfloat16)
    levels = lax.axis_size("rep").bit_length() - 1
    branches = [functools.partial(swapped, axis="rep", distance=level) for level in range(levels)]
    partner = lax.switch(step_index[0] % levels, branches, stepped)
    new_weight = ((stepped.astype(jnp.float32) + partner.astype(jnp.float32)) * 0.5).astype(
        jnp.bfloat16
    )
    return (
        block_out[None],
        query_grad[None],
        key_grad[None],
        value_grad[None],
        new_weight[None],
        new_momentum[None],
    )


def solution(mesh):
    rows = P("rep", "fsdp", None)
    return jax.shard_map(
        on_device,
        mesh=mesh,
        in_specs=(rows, rows, rows, rows, rows, P("rep", "fsdp"), rows, rows, P()),
        out_specs=(rows,) * 6,
        check_vma=False,
    )
```

```python
import functools

import jax
import jax.numpy as jnp
from jax import lax
from jax.experimental import pallas as pl
from jax.experimental.pallas import tpu as pltpu
from jax.sharding import PartitionSpec as P

HEAD_SIZE = 128

momentum_decay = 0.9
learning_rate = 0.0003


def swapped(block, axis, distance):
    count = lax.axis_size(axis)
    route = []
    for low in range(count):
        high = low | 1 << distance
        if high != low and high < count:
            route += [(low, high), (high, low)]
    return lax.ppermute(block, axis, route)


def probabilities(q, k, doc_column, doc_row):
    length = q.shape[0]
    scores = lax.dot_general(
        q, k, (((1,), (1,)), ((), ())), preferred_element_type=jnp.float32
    ) * (HEAD_SIZE ** (-0.5))
    rows = lax.broadcasted_iota(jnp.int32, (length, length), 0)
    columns = lax.broadcasted_iota(jnp.int32, (length, length), 1)
    allowed = (columns <= rows) & (doc_column == doc_row)
    scores = jnp.where(allowed, scores, -jnp.inf)
    exponents = jnp.exp(scores - jnp.max(scores, axis=-1, keepdims=True))
    return exponents / jnp.sum(exponents, axis=-1, keepdims=True)


def forward_kernel(q_ref, k_ref, v_ref, doc_column_ref, doc_row_ref, context_ref):
    for head in range(q_ref.shape[1] // HEAD_SIZE):
        cut = slice(head * HEAD_SIZE, (head + 1) * HEAD_SIZE)
        probs = probabilities(q_ref[:, cut], k_ref[:, cut], doc_column_ref[...], doc_row_ref[...])
        context_ref[:, cut] = jnp.dot(
            probs.astype(jnp.bfloat16), v_ref[:, cut], preferred_element_type=jnp.float32
        ).astype(jnp.bfloat16)


def backward_kernel(
    q_ref, k_ref, v_ref, grad_ref, doc_column_ref, doc_row_ref, dq_ref, dk_ref, dv_ref
):
    for head in range(q_ref.shape[1] // HEAD_SIZE):
        cut = slice(head * HEAD_SIZE, (head + 1) * HEAD_SIZE)
        q, k, v, grad = q_ref[:, cut], k_ref[:, cut], v_ref[:, cut], grad_ref[:, cut]
        probs = probabilities(q, k, doc_column_ref[...], doc_row_ref[...])
        dv_ref[:, cut] = lax.dot_general(
            probs.astype(jnp.bfloat16),
            grad,
            (((0,), (0,)), ((), ())),
            preferred_element_type=jnp.float32,
        ).astype(jnp.bfloat16)
        prob_grad = lax.dot_general(
            grad, v, (((1,), (1,)), ((), ())), preferred_element_type=jnp.float32
        )
        row_delta = jnp.sum(prob_grad * probs, axis=-1, keepdims=True)
        score_grad = (probs * (prob_grad - row_delta) * (HEAD_SIZE ** (-0.5))).astype(jnp.bfloat16)
        dq_ref[:, cut] = jnp.dot(score_grad, k, preferred_element_type=jnp.float32).astype(
            jnp.bfloat16
        )
        dk_ref[:, cut] = lax.dot_general(
            score_grad, q, (((0,), (0,)), ((), ())), preferred_element_type=jnp.float32
        ).astype(jnp.bfloat16)


def per_head(kernel, arrays, doc_block, outputs, matmuls):
    length, width = arrays[0].shape
    step = 2 * HEAD_SIZE if width % (2 * HEAD_SIZE) == 0 else HEAD_SIZE
    block = pl.BlockSpec((length, step), lambda h: (0, h))
    whole = lambda shape: pl.BlockSpec(shape, lambda h: (0, 0))
    result = jax.ShapeDtypeStruct((length, width), jnp.bfloat16)
    return pl.pallas_call(
        kernel,
        grid=(width // step,),
        in_specs=[block] * len(arrays) + [whole((length, 1)), whole((1, length))],
        out_specs=[block] * outputs,
        out_shape=[result] * outputs,
        cost_estimate=pl.CostEstimate(
            flops=4 * matmuls * length * length * width,
            bytes_accessed=(len(arrays) + outputs) * length * width * 2,
            transcendentals=length * length * width // HEAD_SIZE,
        ),
    )(*arrays, doc_block[:, None], doc_block[None, :])


MESH = pl.DeviceIdType.MESH
LANES = 128
PARTS = ((1, 2), (2, 2))


def dot(a, b, ca, cb):
    return lax.dot_general(
        a, b, (((ca,), (cb,)), ((), ())), preferred_element_type=jnp.float32
    )


def step_order(n, chunks):
    order = [(p, c) for p in range(2, n) for c in range(chunks)]
    head, ahead = order[: chunks * (n - 3) + 3], order[chunks * (n - 3) + 3 :]
    tail = [(n, 0), ahead[0], (n, 1)] + ahead[1:] + [(n, 2)]
    tail += [(n + 1, 0)]
    for c in range(3, chunks):
        tail += [(n, c), (n + 1, c - 2)]
    tail += [(n + 1, c) for c in range(chunks - 2, chunks)]
    return head + tail


def line_kernel(
    n,
    level,
    q_hbm,
    k_hbm,
    v_hbm,
    res_hbm,
    g_hbm,
    w_hbm,
    mom_hbm,
    doc_hbm,
    rb,
    qb,
    kb,
    vb,
    nb,
    mb,
    wbuf,
    gown,
    gpair,
    ctx,
    ctxp,
    cg,
    cgs,
    acc,
    oacc,
    osend,
    ogot,
    rs,
    st,
    pr,
    bias,
    own,
    doc_ref,
    ds,
    hs,
    ws,
    gs,
    ms,
    ys,
    xg_s,
    xg_r,
    xc_s,
    xc_r,
    xb_s,
    xb_r,
    xo_s,
    xo_r,
    zs,
    zr,
    fs,
    fr,
    ps,
    pr_r,
):
    units, chunks, rows, wide = wbuf.shape
    size = HEAD_SIZE
    tokens, heads = qb.shape[0], qb.shape[1] // size
    per = heads // n
    coarse, fine = PARTS[min(level, 1)]
    scale = HEAD_SIZE ** (-0.5)
    me = lax.axis_index("fsdp")
    rep = lax.axis_index("rep")
    z = lax.div(me, 2)
    x = lax.rem(me, 2)
    pair = me + 1 - 2 * x
    at_end = (z == 0) | (z == n - 1)

    bit = lax.rem(lax.div(rep, 1 << level), 2)
    partner = rep + (1 << level) - (2 << level) * bit

    def lanes(c, width):
        return pl.ds(pl.multiple_of(c * width, width), width)

    def own_rows(u):
        return pl.ds(pl.multiple_of((2 * u + x) * rows, 16), rows)

    def pair_rows(u):
        return pl.ds(pl.multiple_of((2 * u + 1 - x) * rows, 16), rows)

    def each_part(c, body):
        @pl.when(c < chunks - 1)
        def _():
            each(coarse, lambda s: body(c, s, rows // coarse))

        @pl.when(c == chunks - 1)
        def _():
            each(fine, lambda s: body(c, s, rows // fine))

    def cut_rows(s, part):
        return pl.ds(pl.multiple_of(s * part, 16), part)

    def head_rows(h):
        return pl.ds(pl.multiple_of(h * size, size), size)

    def load_head(i, h):
        src = (q_hbm, k_hbm, v_hbm)[i]
        dst = (qb, kb, vb)[i]
        return pltpu.make_async_copy(src.at[:, lanes(h, size)], dst.at[:, lanes(h, size)], hs.at[i, h])

    def load_w(c):
        return pltpu.make_async_copy(w_hbm.at[:, lanes(c, wide)], wbuf.at[z, c], ws.at[c])

    def load_g(c):
        return pltpu.make_async_copy(g_hbm.at[:, lanes(c, wide)], gown.at[c], gs.at[c])

    def load_m(c):
        return pltpu.make_async_copy(mom_hbm.at[:, lanes(c, wide)], mb.at[:, lanes(c, wide)], ms.at[c])

    def load_y(c):
        return pltpu.make_async_copy(res_hbm.at[:, lanes(c, wide)], rb.at[:, lanes(c, wide)], ys.at[c])

    def to_pair(src, dst, send, recv):
        return pltpu.make_async_remote_copy(
            src_ref=src,
            dst_ref=dst,
            send_sem=send,
            recv_sem=recv,
            device_id={"fsdp": pair},
            device_id_type=MESH,
        )

    def x_grad(c):
        return to_pair(g_hbm.at[:, lanes(c, wide)], gpair.at[c], xg_s.at[c], xg_r.at[c])

    def x_context(u):
        return to_pair(ctx.at[pair_rows(u), :], ctxp.at[u], xc_s.at[u], xc_r.at[u])

    def x_back(u):
        return to_pair(cgs.at[u], cg.at[own_rows(u), :], xb_s.at[u], xb_r.at[u])

    def x_out(c):
        return to_pair(osend.at[c], ogot.at[c], xo_s.at[c], xo_r.at[c])

    def along(d, p, c, src, dst):
        return pltpu.make_async_remote_copy(
            src_ref=src,
            dst_ref=dst,
            send_sem=zs.at[d, p - 1, c],
            recv_sem=zr.at[d, p - 1, c],
            device_id={"fsdp": me + 2 - 4 * d},
            device_id_type=MESH,
        )

    def along_last(d, c, s, part, src, dst):
        return pltpu.make_async_remote_copy(
            src_ref=src.at[cut_rows(s, part), :],
            dst_ref=dst.at[cut_rows(s, part), :],
            send_sem=fs.at[d, c, s],
            recv_sem=fr.at[d, c, s],
            device_id={"fsdp": me + 2 - 4 * d},
            device_id_type=MESH,
        )

    def place(d):
        return z + d * (n - 1 - 2 * z)

    def swap(c, s, part):
        return pltpu.make_async_remote_copy(
            src_ref=st.at[c, cut_rows(s, part), :],
            dst_ref=pr.at[c, cut_rows(s, part), :],
            send_sem=ps.at[c, s],
            recv_sem=pr_r.at[c, s],
            device_id={"rep": partner},
            device_id_type=MESH,
        )

    def block_at(i):
        return jnp.where(2 * z < n, n - 1 - i, i)

    def each(count, body):
        def run(i, carry):
            body(i)
            return carry

        lax.fori_loop(0, count, run, 0)

    def start_loads(i):
        u = block_at(i)

        def one(hh):
            for a in range(3):
                load_head(a, u * per + hh).start()

        each(per, one)

    barrier = pltpu.get_barrier_semaphore()
    pl.semaphore_signal(barrier, inc=1, device_id={"fsdp": pair}, device_id_type=MESH)
    pl.semaphore_signal(barrier, inc=1, device_id={"rep": partner}, device_id_type=MESH)

    @pl.when(z > 0)
    def _():
        pl.semaphore_signal(barrier, inc=1, device_id={"fsdp": me - 2}, device_id_type=MESH)

    @pl.when(z < n - 1)
    def _():
        pl.semaphore_signal(barrier, inc=1, device_id={"fsdp": me + 2}, device_id_type=MESH)

    pl.semaphore_wait(barrier, 2 + jnp.where(at_end, 1, 2))

    def first_sends(c):
        def one(d):
            @pl.when(place(d) < n - 1)
            def _():
                along(d, 1, c, w_hbm.at[:, lanes(c, wide)], wbuf.at[z, c]).start()

        each(2, one)

    each(chunks, first_sends)
    x_grad(0).start()
    load_doc = pltpu.make_async_copy(doc_hbm, doc_ref, ds)
    load_doc.start()
    each(n, start_loads)

    def other_loads(c):
        load_g(c).start()
        load_w(c).start()
        load_m(c).start()
        load_y(c).start()

    each(chunks, other_loads)

    load_doc.wait()
    row_ids = jnp.broadcast_to(doc_ref[...], (tokens, tokens))
    column_ids = jnp.transpose(row_ids)
    r = lax.broadcasted_iota(jnp.int32, (tokens, tokens), 0)
    s = lax.broadcasted_iota(jnp.int32, (tokens, tokens), 1)
    bias[...] = jnp.where((s <= r) & (row_ids == column_ids), 0.0, -jnp.inf)

    blocks = tokens // LANES

    def probabilities_of(q, k, i):
        seen = (i + 1) * LANES
        scores = dot(q[i * LANES : seen], k[:seen], 1, 1) * scale
        scores = scores + bias[i * LANES : seen, :seen]
        exponents = jnp.exp(scores - jnp.max(scores, axis=-1, keepdims=True))
        return exponents * (1.0 / jnp.sum(exponents, axis=-1, keepdims=True))

    def forward_head(h):
        cut_h = lanes(h, size)
        q, k, v = qb[:, cut_h], kb[:, cut_h], vb[:, cut_h]
        parts = []
        for i in range(blocks):
            probs = probabilities_of(q, k, i).astype(jnp.bfloat16)
            parts.append(dot(probs, v[: (i + 1) * LANES], 1, 0))
        context = jnp.concatenate(parts, axis=0)
        ctx[head_rows(h), :] = jnp.transpose(context).astype(jnp.bfloat16)

    def forward_block(i):
        u = block_at(i)

        def one(hh):
            h = u * per + hh
            for a in range(3):
                load_head(a, h).wait()
            forward_head(h)

        each(per, one)
        x_context(u).start()

        @pl.when(i == 0)
        def _():
            each(chunks - 1, lambda c: x_grad(c + 1).start())

    each(n, forward_block)

    def wait_loads(c):
        load_g(c).wait()
        load_w(c).wait()
        load_m(c).wait()
        load_y(c).wait()

    each(chunks, wait_loads)

    def backward_head(h):
        cut_h = lanes(h, size)
        q, k, v = qb[:, cut_h], kb[:, cut_h], vb[:, cut_h]
        grad = jnp.transpose(cg[head_rows(h), :].astype(jnp.float32)).astype(jnp.bfloat16)
        low, score_grads, parts = [], [], []
        for i in range(blocks):
            seen = (i + 1) * LANES
            probs = probabilities_of(q, k, i)
            low.append(probs.astype(jnp.bfloat16))
            prob_grad = dot(grad[i * LANES : seen], v[:seen], 1, 1)
            row_delta = jnp.sum(prob_grad * probs, axis=-1, keepdims=True)
            score_grad = (probs * (prob_grad - row_delta) * scale).astype(jnp.bfloat16)
            score_grads.append(score_grad)
            parts.append(dot(score_grad, k[:seen], 1, 0))
        for i in range(blocks):
            cut = slice(i * LANES, (i + 1) * LANES)
            qb[cut, cut_h] = parts[i].astype(jnp.bfloat16)
        for j in range(blocks):
            cut = slice(j * LANES, (j + 1) * LANES)
            scores_j = jnp.concatenate([b[:, cut] for b in score_grads[j:]], axis=0)
            probs_j = jnp.concatenate([b[:, cut] for b in low[j:]], axis=0)
            kb[cut, cut_h] = dot(scores_j, q[j * LANES :], 0, 0).astype(jnp.bfloat16)
            vb[cut, cut_h] = dot(probs_j, grad[j * LANES :], 0, 0).astype(jnp.bfloat16)

    def backward_heads(u, low, high):
        @pl.when(low == 0)
        def _():
            x_back(u).wait_recv()

        def one(hh, carry):
            backward_head(u * per + hh)
            return carry

        lax.fori_loop(low, high, one, 0)

    def weight_part(u, c):
        return dot(ctx[own_rows(u), :], gown[c], 1, 0) + dot(ctxp[u], gpair[c], 1, 0)

    def unit_chunk(i, u, c):
        weight = wbuf[u, c]
        for side in range(2):
            left = ctx[own_rows(u), :] if side == 0 else ctxp[u]
            grad = gown[c] if side == 0 else gpair[c]
            before = jnp.where(u == z, 0.0, oacc[side, c])
            oacc[side, c] = before + dot(left, weight, 0, 0)
            before = jnp.where(c == 0, 0.0, acc[i, side])
            acc[i, side] = before + dot(weight, grad, 1, 1)

        @pl.when(c == chunks - 1)
        def _():
            cgs[u] = acc[i, 1].astype(jnp.bfloat16)
            cg[own_rows(u), :] = acc[i, 0].astype(jnp.bfloat16)
            x_back(u).start()

    far = jnp.where(2 * z < n, z + 2, z - 2)

    def finish_part(c, s, part):
        def arrived(d):
            @pl.when(place(d) > 0)
            def _():
                along_last(d, c, s, part, rs.at[0, 0], rs.at[0, 0]).wait_recv()

        each(2, arrived)
        cut, across = cut_rows(s, part), lanes(c, wide)
        total = own[cut, :]
        total = total + jnp.where(z > 0, rs[z, c, cut, :].astype(jnp.float32), 0.0)
        total = total + jnp.where(z < n - 1, rs[n, c, cut, :].astype(jnp.float32), 0.0)
        moment = momentum_decay * mb[cut, across] + total
        mb[cut, across] = moment
        stepped = wbuf[z, c, cut, :].astype(jnp.float32) - learning_rate * moment
        st[c, cut, :] = stepped.astype(jnp.bfloat16)
        swap(c, s, part).start()
        a, b, e = min(2, per), min(3, per), min(4, per)
        tip = coarse - 1
        u, low, high = pick(
            [
                (at_end & (c == 0) & (s == tip), (far, 0, per)),
                (at_end & (c == chunks - 3) & (s == tip), (last, 0, a)),
                (at_end & (c == chunks - 2) & (s == 0), (last, a, e if coarse == 1 else b)),
                (at_end & (c == chunks - 2) & (s == 1), (last, b, e)),
                (at_end & (c == chunks - 1) & (s == (fine - 1 if level else 0)), (last, e, per)),
                (~at_end & (c == 0) & (s == tip), (z + 1, 0, per)),
                (~at_end & (c == 1) & (s == tip), (far, 0, per)),
            ]
        )

        @pl.when(u >= 0)
        def _():
            backward_heads(u, low, high)

    def average(c, s, part):
        cut = cut_rows(s, part)
        swap(c, s, part).wait()
        other = pr[c, cut, :].astype(jnp.float32)
        mean = (st[c, cut, :].astype(jnp.float32) + other) * 0.5
        nb[cut, lanes(c, wide)] = mean.astype(jnp.bfloat16)

    def pick(cases):
        values = (-1, 0, 0)
        for condition, choice in cases:
            values = tuple(jnp.where(condition, a, b) for a, b in zip(choice, values))
        return values

    last = n - 1 - z
    first_side = jnp.where(z > 0, z - 1, z + 1)

    def early_sent(c):
        def line(d):
            @pl.when(place(d) < n - 1)
            def _():
                for p in range(1, n):
                    along(d, p, c, rs.at[0, 0], rs.at[0, 0]).wait_send()

        each(2, line)
        x_grad(c).wait_send()

    def unit_sent(u):
        x_context(u).wait_send()
        x_back(u).wait_send()

    def last_sent(c):
        def line(d):
            @pl.when(place(d) < n - 1)
            def _():
                each_part(
                    c,
                    lambda c, s, part: along_last(
                        d, c, s, part, rs.at[0, 0], rs.at[0, 0]
                    ).wait_send(),
                )

        each(2, line)
        x_out(c).wait_send()

    def finish(c):
        own[...] = weight_part(z, c)
        if level == 0:

            @pl.when(c == chunks - 1)
            def _():
                each(chunks, early_sent)
                each(n, unit_sent)

            @pl.when(c > 0)
            def _():
                each_part(c - 1, average)
                last_sent(c - 1)
                finish_out(c - 1)

            @pl.when(c == chunks - 1)
            def _():
                finish_out(c)

            each_part(c, finish_part)
            return

        each_part(c, finish_part)

        @pl.when(c < chunks - 2)
        def _():
            finish_out(c)

        @pl.when((c > 0) & (c < chunks - 2))
        def _():
            each_part(c - 1, average)
            last_sent(c - 1)

        @pl.when(c == chunks - 1)
        def _():
            finish_out(chunks - 2)
            finish_out(chunks - 1)
            for i in (3, 2):
                each_part(chunks - i, average)
                last_sent(chunks - i)
            each(chunks, early_sent)
            each(n, unit_sent)

    def finish_out(c):
        x_out(c).wait_recv()
        across = lanes(c, wide)
        total_out = rb[:, across].astype(jnp.float32) + oacc[0, c]
        rb[:, across] = (total_out + ogot[c].astype(jnp.float32)).astype(jnp.bfloat16)

    order = step_order(n, chunks)

    def step(t):
        code = 0
        for i, (p, c) in enumerate(order):
            code = jnp.where(t == i, p * chunks + c, code)
        p = lax.div(code, chunks)
        c = lax.rem(code, chunks)

        @pl.when(p <= n)
        def _():
            def arrived(d):
                @pl.when(place(d) > 0)
                def _():
                    along(d, p - 1, c, rs.at[0, 0], rs.at[0, 0]).wait_recv()

            each(2, arrived)

            def forward(d):
                zz = place(d)

                @pl.when((zz < n - 1) & (p <= zz + 1))
                def _():
                    u = zz + 1 - p
                    u = u + d * (n - 1 - 2 * u)
                    along(d, p, c, wbuf.at[u, c], wbuf.at[u, c]).start()

            each(2, forward)

            @pl.when(p == 2)
            def _():
                x_grad(c).wait_recv()

                @pl.when(c == 0)
                def _():
                    x_context(block_at(0)).wait_recv()

            @pl.when((p == 3) & (c == 0))
            def _():
                each(n - 1, lambda i: x_context(block_at(i + 1)).wait_recv())

            def reduce(d):
                zz = place(d)

                @pl.when((zz < n - 1) & (p > zz + 1))
                def _():
                    b = zz + 1 + n - p
                    b = b + d * (n - 1 - 2 * b)
                    before = jnp.where(zz > 0, rs[b, c].astype(jnp.float32), 0.0)
                    rs[b, c] = (before + weight_part(b, c)).astype(jnp.bfloat16)

                    @pl.when(p < n)
                    def _():
                        along(d, p, c, rs.at[b, c], rs.at[b, c]).start()

                    @pl.when(p == n)
                    def _():
                        slot = jnp.where(d == 1, n, b)
                        each_part(
                            c,
                            lambda c, s, part: along_last(
                                d, c, s, part, rs.at[b, c], rs.at[slot, c]
                            ).start(),
                        )

            each(2, reduce)

        @pl.when((p == 3) | (p == 4))
        def _():
            def unit(i):
                u, low, high = pick(
                    [
                        ((i == 0) & (p == 3) & (c == 0), (z, 0, chunks)),
                        ((i == 0) & (p == 3) & (c == 1), (z - 1, 0, chunks)),
                        ((i == 0) & (p == 3) & (c == 2) & (z < n - 1), (z + 1, 0, chunks)),
                        ((i == 1) & (p == 3), (far, c, c + 1)),
                        ((i == 1) & (p == 4) & at_end, (last, c, c + 1)),
                    ]
                )
                slot = jnp.where(i == 0, 0, p - 2)

                @pl.when(u >= 0)
                def _():
                    def one(cc, carry):
                        unit_chunk(slot, u, cc)
                        return carry

                    lax.fori_loop(low, high, one, 0)

            each(2, unit)

        @pl.when(p == n)
        def _():
            osend[c] = oacc[1, c].astype(jnp.bfloat16)
            x_out(c).start()

            @pl.when((c == 1) | (c == 2))
            def _():
                backward_heads(jnp.where(c == 1, z, first_side), 0, per)

        @pl.when(p == n + 1)
        def _():
            finish(c)

    each(len(order), step)
    each_part(chunks - 1, average)

    last_sent(chunks - 1)


def write_kernel(*refs):
    count = len(refs) // 2
    sems = refs[-1]
    copies = [
        pltpu.make_async_copy(refs[i], refs[count + i], sems.at[i]) for i in range(count)
    ]
    for copy in copies:
        copy.start()
    for copy in copies:
        copy.wait()


def line_shape(count, levels, tokens, features, rows, columns):
    n = count // 2
    heads = features // HEAD_SIZE
    wide = 4 * LANES
    fits = (
        count % 2 == 0
        and n == 4
        and levels >= 1
        and tokens % LANES == 0
        and rows % 16 == 0
        and heads % n == 0
        and 2 * rows * n == features
        and columns % wide == 0
        and columns // wide >= 5
        and all(rows % (16 * part) == 0 for parts in PARTS for part in parts)
    )
    return (n, wide) if fits else None


def on_line(
    n, wide, level, query, key, value, residual, out_grad, doc_ids, weight, momentum
):
    tokens, features = query.shape
    rows, columns = weight.shape
    chunks = columns // wide
    heads = features // HEAD_SIZE
    any_space = pl.BlockSpec(memory_space=pl.ANY)
    in_vmem = pl.BlockSpec(memory_space=pltpu.VMEM)
    fine = max(PARTS[min(level, 1)])
    low, full = jnp.bfloat16, jnp.float32
    dma = pltpu.SemaphoreType.DMA
    like = lambda a: jax.ShapeDtypeStruct(a.shape, a.dtype)
    held = pl.pallas_call(
        functools.partial(line_kernel, n, level),
        in_specs=[any_space] * 8,
        out_specs=[in_vmem] * 6,
        out_shape=[
            pltpu.VMEM(a.shape, a.dtype)
            for a in (residual, query, key, value, weight, momentum)
        ],
        scratch_shapes=[
            pltpu.VMEM((n, chunks, rows, wide), low),
            pltpu.VMEM((chunks, tokens, wide), low),
            pltpu.VMEM((chunks, tokens, wide), low),
            pltpu.VMEM((features, tokens), low),
            pltpu.VMEM((n, rows, tokens), low),
            pltpu.VMEM((features, tokens), low),
            pltpu.VMEM((n, rows, tokens), low),
            pltpu.VMEM((3, 2, rows, tokens), full),
            pltpu.VMEM((2, chunks, tokens, wide), full),
            pltpu.VMEM((chunks, tokens, wide), low),
            pltpu.VMEM((chunks, tokens, wide), low),
            pltpu.VMEM((n + 1, chunks, rows, wide), low),
            pltpu.VMEM((chunks, rows, wide), low),
            pltpu.VMEM((chunks, rows, wide), low),
            pltpu.VMEM((tokens, tokens), full),
            pltpu.VMEM((rows, wide), full),
            pltpu.VMEM((1, tokens), jnp.int32),
            dma(()),
            dma((3, heads)),
            dma((chunks,)),
            dma((chunks,)),
            dma((chunks,)),
            dma((chunks,)),
            dma((chunks,)),
            dma((chunks,)),
            dma((n,)),
            dma((n,)),
            dma((n,)),
            dma((n,)),
            dma((chunks,)),
            dma((chunks,)),
            dma((2, n - 1, chunks)),
            dma((2, n - 1, chunks)),
            dma((2, chunks, fine)),
            dma((2, chunks, fine)),
            dma((chunks, fine)),
            dma((chunks, fine)),
        ],
        compiler_params=pltpu.CompilerParams(
            collective_id=level, has_side_effects=True, vmem_limit_bytes=50 << 20
        ),
    )(
        query,
        key,
        value,
        residual,
        out_grad,
        weight,
        momentum,
        doc_ids,
    )
    return pl.pallas_call(
        write_kernel,
        in_specs=[any_space] * 6,
        out_specs=[any_space] * 6,
        out_shape=[like(a) for a in (residual, query, key, value, weight, momentum)],
        scratch_shapes=[dma((6,))],
        compiler_params=pltpu.CompilerParams(vmem_limit_bytes=1 << 20),
    )(*held)


def on_device(
    query_rows,
    key_rows,
    value_rows,
    residual_in,
    out_grad,
    doc_ids,
    out_weight,
    momentum,
    step_index,
):
    count = lax.axis_size("fsdp")
    shape = line_shape(
        count,
        lax.axis_size("rep").bit_length() - 1,
        query_rows.shape[1],
        query_rows.shape[2],
        out_weight.shape[1],
        out_weight.shape[2],
    )
    if shape is not None:
        arrays = (query_rows, key_rows, value_rows, residual_in, out_grad)
        levels = lax.axis_size("rep").bit_length() - 1
        results = lax.switch(
            lax.rem(step_index[0].astype(jnp.uint32), jnp.uint32(levels)).astype(jnp.int32),
            [functools.partial(on_line, *shape, level) for level in range(levels)],
            *[a[0] for a in arrays],
            doc_ids,
            out_weight[0],
            momentum[0],
        )
        return tuple(r[None] for r in results)
    side = lax.axis_index("fsdp") % 2
    groups = [[i for i in range(count) if i % 2 == s] for s in range(2)]
    pair = [(i, i ^ 1) for i in range(count)]
    first = side == 0
    query, key, value = query_rows[0], key_rows[0], value_rows[0]
    weight_shard = out_weight[0]
    own_grad = out_grad[0]
    rows = weight_shard.shape[0]
    gathered = lax.all_gather(
        weight_shard, "fsdp", axis=0, tiled=True, axis_index_groups=groups
    )
    pair_grad = lax.ppermute(own_grad, "fsdp", pair)
    (context,) = per_head(forward_kernel, (query, key, value), doc_ids[0], 1, 2)

    def half(array, which):
        return jnp.concatenate(
            [array[:, j * rows : (j + 1) * rows] for j in range(which, count, 2)], axis=1
        )

    low, high = half(context, 0), half(context, 1)
    own_context = jnp.where(first, low, high)
    pair_context = lax.ppermute(jnp.where(first, high, low), "fsdp", pair)

    def outer(left, right):
        return lax.dot_general(
            left, right, (((0,), (0,)), ((), ())), preferred_element_type=jnp.float32
        )

    weight_term = (outer(own_context, own_grad) + outer(pair_context, pair_grad)).astype(
        jnp.bfloat16
    )
    weight_grad = lax.psum_scatter(
        weight_term, "fsdp", scatter_dimension=0, tiled=True, axis_index_groups=groups
    ).astype(jnp.float32)

    def back(grad):
        return lax.dot_general(
            grad, gathered, (((1,), (1,)), ((), ())), preferred_element_type=jnp.float32
        ).astype(jnp.bfloat16)

    got_back = lax.ppermute(back(pair_grad), "fsdp", pair)
    pair_out = jnp.dot(pair_context, gathered, preferred_element_type=jnp.float32)
    got_out = lax.ppermute(pair_out.astype(jnp.bfloat16), "fsdp", pair)
    own_back = back(own_grad)
    even = jnp.where(first, own_back, got_back)
    odd = jnp.where(first, got_back, own_back)
    pieces = []
    for j in range(count // 2):
        cut = slice(j * rows, (j + 1) * rows)
        pieces += [even[:, cut], odd[:, cut]]
    context_grad = jnp.concatenate(pieces, axis=1)
    query_grad, key_grad, value_grad = per_head(
        backward_kernel, (query, key, value, context_grad), doc_ids[0], 3, 5
    )
    own_out = jnp.dot(own_context, gathered, preferred_element_type=jnp.float32)
    block_out = (
        residual_in[0].astype(jnp.float32) + own_out + got_out.astype(jnp.float32)
    ).astype(jnp.bfloat16)

    new_momentum = momentum_decay * momentum[0] + weight_grad
    stepped = (weight_shard.astype(jnp.float32) - learning_rate * new_momentum).astype(jnp.bfloat16)
    levels = lax.axis_size("rep").bit_length() - 1
    branches = [functools.partial(swapped, axis="rep", distance=level) for level in range(levels)]
    partner = lax.switch(step_index[0] % levels, branches, stepped)
    new_weight = ((stepped.astype(jnp.float32) + partner.astype(jnp.float32)) * 0.5).astype(
        jnp.bfloat16
    )
    return (
        block_out[None],
        query_grad[None],
        key_grad[None],
        value_grad[None],
        new_weight[None],
        new_momentum[None],
    )


def solution(mesh):
    rows = P("rep", "fsdp", None)
    return jax.shard_map(
        on_device,
        mesh=mesh,
        in_specs=(rows, rows, rows, rows, rows, P("rep", "fsdp"), rows, rows, P()),
        out_specs=(rows,) * 6,
        check_vma=False,
    )
```
